32 devices in a mesh: seq: 8 (over y, x, core), head: 4 (over z).
Axes of the slice: x: 2, y: 2, z: 4, core: 2. Of those that a mesh axis runs over, the one named last changes fastest.
Arguments:
- query: bfloat16 [4096, 4096], P('seq', 'head'), may hold values from -6 to 6
- keys: bfloat16 [4096, 4096], P('seq', 'head'), may hold values from -6 to 6
- values: bfloat16 [4096, 4096], P('seq', 'head'), may hold values from -6 to 6
- log_decay: float32 [32, 4096], P('head', 'seq'), may hold values from -1 to 0, as said below
- beta: float32 [32, 4096], P('head', 'seq'), may hold values from 0.002 to 0.1
- level_weights: float32 [7, 32, 4096], P(None, 'head', 'seq'), may hold values from 0.25 to 4
- norm_gain: float32 [4096], P('head'), may hold values from 0.1 to 1.9
- out_weight: bfloat16 [4096, 4096], P('head'), may hold values from -0.09375 to 0.09375
Outputs:
- mixed: bfloat16 [4096, 4096], P(('seq', 'head'))
The draws below stay inside these ranges and needn't reach their ends.
Inputs may be any that keep to these rules, and one draw needn't show every extreme that they name: log_decay is negative everywhere.
All inputs are finite; a program needn't handle non-finite values.
Results may differ from the reference program's by a relative error of at most 0.014.
Values may be sent and summed in bfloat16 or wider, within the bound.
A program may use at most 128 MiB of HBM per device.

```python
import math
import jax
import jax.numpy as jnp
from jax import lax

D = 4096
H = 32
DK = 128
DV = 128
TOK_DEV = 512
BLK = 64
PATH_SYMBOLS = 4096
BPD = 8
LOGB = 3
LOGS = 3
LEVELS = 7
N_SEQ = 8
N_HEAD = 4


def draw_log_decay(key, part):
    complete_lookup_lines = jax.random.split(key, 5)
    share = 0.5
    quick = jax.random.uniform(complete_lookup_lines[0], (H, 1)) < share
    slow_rate = math.log(0.3) / PATH_SYMBOLS
    quick_rate = -1.0 / 40.0
    starting_quantity = jnp.where(quick, quick_rate, slow_rate)
    approximate_guess = jax.random.uniform(complete_lookup_lines[1], (H, PATH_SYMBOLS), jnp.float32, 0.5, 1.5)
    multiplier_coefficient = jnp.exp(jax.random.uniform(complete_lookup_lines[2], (H, PATH_SYMBOLS // TOK_DEV), jnp.float32, -math.log(2.0), math.log(2.0)))
    multiplier_coefficient = jnp.repeat(multiplier_coefficient, TOK_DEV, axis=1)
    clustered_sets = jax.random.uniform(complete_lookup_lines[3], (1, PATH_SYMBOLS)) < 6.0 / PATH_SYMBOLS
    discarded_tier = jnp.log(jax.random.uniform(complete_lookup_lines[4], (H, PATH_SYMBOLS), jnp.float32, 0.5, 0.8))
    concluding_result = starting_quantity * approximate_guess * multiplier_coefficient + jnp.where(clustered_sets, discarded_tier, 0.0)
    return concluding_result.astype(jnp.float32)


def steps_of(rng, extent, cuts, least, largest):
    def one(dim, shards_of):
        steps = jax.random.uniform(jax.random.fold_in(jax.random.fold_in(rng, 6), dim), (shards_of,), jnp.float32, least / len(cuts), largest / len(cuts))
        return jnp.repeat(jnp.exp(steps), extent[dim] // shards_of).reshape((-1,) + (1,) * (len(extent) - dim - 1))

    loudness = one(*cuts[0])
    for cut in cuts[1:]:
        loudness = loudness * one(*cut)
    return loudness


def normal_values(key, shape, scale, reach, cuts=(), kind=jnp.bfloat16):
    drawn = scale * jax.random.normal(key, shape, jnp.float32)
    if cuts:
        drawn = drawn * steps_of(key, shape, cuts, -0.22, 0.18)
    return jnp.clip(drawn, -reach, reach).astype(kind)


def setup_inputs(seed: int = 0) -> dict:
    seeds = jax.random.split(jax.random.key(seed), 9)
    return {
        "query": normal_values(seeds[0], (PATH_SYMBOLS, H * DK), 1.0, 6.0, ((0, 8), (1, 4))),
        "keys": normal_values(seeds[1], (PATH_SYMBOLS, H * DK), 1.0, 6.0, ((0, 8), (1, 4))),
        "values": normal_values(seeds[2], (PATH_SYMBOLS, H * DV), 1.0, 6.0, ((0, 8), (1, 4))),
        "log_decay": draw_log_decay(jax.random.fold_in(seeds[8], 71), 0),
        "beta": jnp.clip(jnp.exp(math.log(0.1) - 3.912023 * jax.random.uniform(seeds[4], (H, PATH_SYMBOLS), jnp.float32) ** steps_of(seeds[4], (H, PATH_SYMBOLS), ((0, 4), (1, 8)), -0.2, 0.2)), 0.002, 0.1),
        "level_weights": jnp.clip(jnp.exp(math.log(4.0) - 2.7725887 * jax.random.uniform(seeds[5], (LEVELS, H, PATH_SYMBOLS), jnp.float32) ** steps_of(seeds[5], (LEVELS, H, PATH_SYMBOLS), ((1, 4), (2, 8)), -0.2, 0.2)), 0.25, 4.0),
        "norm_gain": jnp.clip(1.0 + 0.18 * jax.random.normal(seeds[6], (H * DV,), jnp.float32), 0.1, 1.9),
        "out_weight": normal_values(seeds[7], (H * DV, D), (H * DV) ** -0.5, 0.09375, ((0, 4),)),
    }


def product(form, left, right):
    return jnp.einsum(form, left, right, precision=lax.Precision.HIGHEST)

def unit_rows(matrix):
    return matrix * lax.rsqrt(lax.optimization_barrier(jnp.sum(matrix * matrix, -1, keepdims=True)) + 1e-06)

def block_terms(query, keys, values, log_gate, beta):
    width = log_gate.shape[-1]
    running = jnp.cumsum(log_gate, -1)
    places = jnp.arange(width)
    on_or_below = places[:, None] >= places[None, :]
    below_diag = places[:, None] > places[None, :]
    gap = running[..., :, None] - running[..., None, :]
    decay = jnp.where(on_or_below, jnp.exp(jnp.where(on_or_below, gap, 0.0)), 0.0)
    key_dots = product('bik,bjk->bij', keys, keys)
    unit_lower = jnp.where(below_diag, beta[..., :, None] * decay * key_dots, 0.0) + jnp.eye(width, dtype=jnp.float32)
    mixer = decay * product('bik,bjk->bij', query, keys)
    fresh = jax.scipy.linalg.solve_triangular(unit_lower, beta[..., None] * values, lower=True, unit_diagonal=True)
    gamma = jnp.exp(running)
    carried = jax.scipy.linalg.solve_triangular(unit_lower, (beta * gamma)[..., None] * keys, lower=True, unit_diagonal=True)
    local_out = product('bij,bjv->biv', mixer, fresh)
    query_eff = gamma[..., None] * query - product('bij,bjk->bik', mixer, carried)
    tail_keys = jnp.exp(running[..., -1:] - running)[..., None] * keys
    end_state = product('bjk,bjv->bkv', tail_keys, fresh)
    identity = jnp.eye(keys.shape[-1], dtype=jnp.float32)
    transit = gamma[..., -1][..., None, None] * identity - product('bjk,bjl->bkl', tail_keys, carried)
    return (local_out, query_eff, end_state, transit)

def fenwick_step(levels, transit, end_state, index):
    depth = levels.shape[0]
    spread = jnp.bitwise_xor(index, index + 1)
    highest = jnp.sum(spread >> jnp.arange(depth + 2, dtype=jnp.int32) > 0).astype(jnp.int32)
    order = jnp.arange(1, depth + 1, dtype=jnp.int32).reshape((depth,) + (1,) * (levels.ndim - 1))
    moved = product('...kl,n...lv->n...kv', transit, levels)
    below = lax.optimization_barrier(jnp.sum(jnp.where(order < highest, moved, 0.0), 0))
    return jnp.where(order > highest, moved, 0.0) + jnp.where(order == highest, below + end_state, 0.0)

def device_pass(query_eff, end_state, transit, weights):
    batch, nblock = (query_eff.shape[0], query_eff.shape[1])
    key_width, value_width = (end_state.shape[2], end_state.shape[3])
    depth = weights.shape[0]
    inputs = (jnp.moveaxis(query_eff, 1, 0), jnp.moveaxis(end_state, 1, 0), jnp.moveaxis(transit, 1, 0), jnp.moveaxis(weights, 2, 0), jnp.arange(nblock, dtype=jnp.int32))

    def advance(carry, item):
        levels, running, total = carry
        query_block, end_block, transit_block, weight_block, index = item
        inner = product('btk,nbkv->nbtv', query_block, levels)
        near = lax.optimization_barrier(jnp.sum(weight_block[..., None] * inner, 0))
        seen = product('btk,bkl->btl', query_block, running)
        levels = fenwick_step(levels, transit_block, end_block, index)
        running = product('bkl,blm->bkm', transit_block, running)
        total = product('bkl,blv->bkv', transit_block, total) + end_block
        return ((levels, running, total), (near, seen))
    start = (jnp.zeros((depth, batch, key_width, value_width), jnp.float32), jnp.broadcast_to(jnp.eye(key_width, dtype=jnp.float32), (batch, key_width, key_width)), jnp.zeros((batch, key_width, value_width), jnp.float32))
    (levels, running, total), (near, seen) = lax.scan(advance, start, inputs)
    return (jnp.moveaxis(near, 0, 1), jnp.moveaxis(seen, 0, 1), running, total)

def head_merge(local_out, near, seen, cross, weights, depth):
    far = product('bntk,jbkv->jbntv', seen, cross)
    far_sum = lax.optimization_barrier(jnp.sum(weights[1 + depth:][..., None] * far, 0))
    return weights[0][..., None] * local_out + near + far_sum

def one_head(query, keys, values, log_gate, beta, weights):
    query_rows = unit_rows(query.astype(jnp.float32)).reshape(N_SEQ * BPD, BLK, DK)
    key_rows = unit_rows(keys.astype(jnp.float32)).reshape(N_SEQ * BPD, BLK, DK)
    value_rows = values.astype(jnp.float32).reshape(N_SEQ * BPD, BLK, DV)
    local_out, query_eff, end_state, transit = block_terms(query_rows, key_rows, value_rows, log_gate.reshape(N_SEQ * BPD, BLK), beta.reshape(N_SEQ * BPD, BLK))
    local_out = local_out.reshape(N_SEQ, BPD, BLK, DV)
    query_eff = query_eff.reshape(N_SEQ, BPD, BLK, DK)
    end_state = end_state.reshape(N_SEQ, BPD, DK, DV)
    transit = transit.reshape(N_SEQ, BPD, DK, DK)
    weights = weights.reshape(LEVELS, N_SEQ, BPD, BLK)
    near, seen, dev_transit, dev_state = device_pass(query_eff, end_state, transit, weights[1:1 + LOGB])

    def chain(levels, item):
        transit_dev, state_dev, index = item
        return (fenwick_step(levels, transit_dev, state_dev, index), levels)
    _, cross = lax.scan(chain, jnp.zeros((LOGS, DK, DV), jnp.float32), (dev_transit, dev_state, jnp.arange(N_SEQ, dtype=jnp.int32)))
    cross = jnp.moveaxis(cross, 0, 1)
    merged = head_merge(local_out, near, seen, cross, weights, LOGB)
    return merged.reshape(PATH_SYMBOLS, DV)

def reference(query, keys, values, log_decay, beta, level_weights, norm_gain, out_weight):
    query_heads = query.reshape(PATH_SYMBOLS, H, DK).transpose(1, 0, 2)
    key_heads = keys.reshape(PATH_SYMBOLS, H, DK).transpose(1, 0, 2)
    value_heads = values.reshape(PATH_SYMBOLS, H, DV).transpose(1, 0, 2)
    weight_heads = level_weights.transpose(1, 0, 2)
    attended = lax.map(lambda item: one_head(*item), (query_heads, key_heads, value_heads, log_decay, beta, weight_heads))
    scaled = attended * lax.rsqrt(lax.optimization_barrier(jnp.mean(attended * attended, -1, keepdims=True)) + 1e-06)
    scaled = scaled * norm_gain.reshape(H, DV)[:, None, :]
    normed = scaled.transpose(1, 0, 2).reshape(PATH_SYMBOLS, H * DV).astype(jnp.bfloat16)
    group = H * DV // N_HEAD
    total = jnp.zeros((PATH_SYMBOLS, D), jnp.float32)
    for member in range(N_HEAD):
        partial_sum = jnp.dot(normed[:, member * group:(member + 1) * group].astype(jnp.float32), out_weight[member * group:(member + 1) * group].astype(jnp.float32), preferred_element_type=jnp.float32)
        rounded = lax.optimization_barrier(partial_sum.astype(jnp.bfloat16))
        total = total + rounded.astype(jnp.float32)
    return total.astype(jnp.bfloat16)
```

```python
import functools

import jax
import jax.numpy as jnp
from jax import lax
from jax.experimental import pallas as pl
from jax.experimental.pallas import tpu as pltpu
from jax.sharding import PartitionSpec as P

BLK = 64
HALF = 256
MESH = pl.DeviceIdType.MESH
F32 = jnp.float32
B16 = jnp.bfloat16


def mm(left, right):
    return jnp.dot(left, right, preferred_element_type=F32)


def mm_t(left, right):
    return lax.dot_general(left, right, (((1,), (1,)), ((), ())), preferred_element_type=F32)


def mm_tl(left, right):
    return lax.dot_general(left, right, (((0,), (0,)), ((), ())), preferred_element_type=F32)


def unit_rows(matrix):
    return matrix * lax.rsqrt(jnp.sum(matrix * matrix, -1, keepdims=True) + 1e-06)


def places(rows, cols):
    return (
        lax.broadcasted_iota(jnp.int32, (rows, cols), 0),
        lax.broadcasted_iota(jnp.int32, (rows, cols), 1),
    )


def unit_lower_inverses(lowers):
    row, col = places(HALF, HALF)

    def same(size):
        return (row // size) == (col // size)

    eye = jnp.where(row == col, 1.0, 0.0)
    ys = [jnp.where(same(16), -low, 0.0) for low in lowers]
    yb = [y.astype(B16) for y in ys]
    y2 = [mm(y, y) for y in yb]
    y2b = [y.astype(B16) for y in y2]
    y3 = [mm(y, z) for y, z in zip(yb, y2b)]
    y4b = [mm(y, y).astype(B16) for y in y2b]
    first = [eye + a + b + c for a, b, c in zip(ys, y2, y3)]
    y8b = [mm(y, y).astype(B16) for y in y4b]
    second = [a + mm(a.astype(B16), y) for a, y in zip(first, y4b)]
    xs = [a + mm(a.astype(B16), y) for a, y in zip(second, y8b)]
    size = 16
    while size < HALF:
        ring = same(2 * size) & jnp.logical_not(same(size))
        xb = [x.astype(B16) for x in xs]
        inner = [
            mm(jnp.where(ring, low, 0.0).astype(B16), x).astype(B16) for low, x in zip(lowers, xb)
        ]
        xs = [x - mm(b, t) for x, b, t in zip(xs, xb, inner)]
        size *= 2
    return [x.astype(B16) for x in xs]


def attention_kernel(
    heads, rounds, depth,
    q_ref, k_ref, v_ref, decay_ref, beta_ref, weight_ref, gain_ref,
    o_ref,
    running, rows, local, seen, own, carry, cross, send, recv, send_sem, recv_sem,
):
    step = pl.program_id(0)
    me = lax.axis_index("seq")
    tokens = q_ref.shape[0]
    width = q_ref.shape[1]

    def partner(r):
        bit = (me // (1 << r)) % 2
        return me + (1 - 2 * bit) * (1 << r), bit

    def copy(r, head):
        return pltpu.make_async_remote_copy(
            src_ref=send.at[r, head],
            dst_ref=recv.at[r, head],
            send_sem=send_sem.at[r, head],
            recv_sem=recv_sem.at[r, head],
            device_id={"seq": partner(r)[0]},
            device_id_type=MESH,
        )

    @pl.when(step == 0)
    def _():
        barrier = pltpu.get_barrier_semaphore()
        for r in range(rounds):
            pl.semaphore_signal(
                barrier, inc=1, device_id={"seq": partner(r)[0]}, device_id_type=MESH
            )
        pl.semaphore_wait(barrier, rounds)
        total = decay_ref[...]
        lane = lax.broadcasted_iota(jnp.int32, total.shape, 1)
        shift = 1
        while shift < tokens:
            total = total + jnp.where(lane >= shift, pltpu.roll(total, shift, 1), 0.0)
            shift *= 2
        running[...] = total
        rows[...] = jnp.zeros_like(rows)

    @pl.when(step < heads)
    def _():
        head = step
        rows[0:1, :] = running[pl.ds(head, 1), :]
        rows[1:2, :] = beta_ref[pl.ds(head, 1), :]
        for level in range(1 + depth):
            rows[2 + level : 3 + level, :] = weight_ref[level, pl.ds(head, 1), :]
        run_row = rows[0:1, :]
        cols = rows[...].T
        run = cols[:, 0:1]
        beta = cols[:, 1:2]
        gamma = jnp.exp(run)
        end = run[tokens - 1 : tokens, :]
        qn = unit_rows(q_ref[...].astype(F32))
        kn = unit_rows(k_ref[...].astype(F32))
        qb = qn.astype(B16)
        kb = kn.astype(B16)
        fresh = (beta * v_ref[...].astype(F32)).astype(B16)
        faded = (beta * gamma * kn).astype(B16)
        pair = jnp.concatenate([fresh, faded], -1)
        tail = (jnp.exp(end - run) * kn).astype(B16)
        row, col = places(HALF, HALF)
        lo, hi = slice(0, HALF), slice(HALF, 2 * HALF)

        def decay(i, j):
            gap = jnp.exp(jnp.minimum(run[i] - run_row[:, j], 0.0))
            return jnp.where(row >= col, gap, 0.0) if i == j else gap

        d00, d10, d11 = decay(lo, lo), decay(hi, lo), decay(hi, hi)
        below = row > col
        l00 = jnp.where(below, beta[lo] * d00 * mm_t(kb[lo], kb[lo]), 0.0)
        l11 = jnp.where(below, beta[hi] * d11 * mm_t(kb[hi], kb[hi]), 0.0)
        l10 = (beta[hi] * d10 * mm_t(kb[hi], kb[lo])).astype(B16)
        m00 = (d00 * mm_t(qb[lo], kb[lo])).astype(B16)
        m11 = (d11 * mm_t(qb[hi], kb[hi])).astype(B16)
        m10 = (d10 * mm_t(qb[hi], kb[lo])).astype(B16)
        x00, x11 = unit_lower_inverses([l00, l11])
        x10 = (-mm(x11, mm(l10, x00).astype(B16))).astype(B16)
        p00 = mm(m00, x00)
        p11 = mm(m11, x11)
        p10 = (mm(m10, x00) + mm(m11, x10)).astype(B16)

        def level_weight(i):
            chosen = cols[i, 1 + depth : 2 + depth]
            for level in range(depth - 2, -1, -1):
                span = BLK << level
                chosen = jnp.where(
                    (row // span) == (col // span), cols[i, 2 + level : 3 + level], chosen
                )
            return chosen

        both = mm(p10, pair[lo])
        local[head, lo, :] = mm((level_weight(lo) * p00).astype(B16), fresh[lo])
        local[head, hi, :] = (
            mm((level_weight(hi) * p11).astype(B16), fresh[hi])
            + cols[hi, 2 + depth : 3 + depth] * both[:, :width]
        )
        seen[head, lo, :] = (gamma[lo] * qn[lo] - mm(p00.astype(B16), faded[lo])).astype(B16)
        seen[head, hi, :] = (
            gamma[hi] * qn[hi] - both[:, width:] - mm(p11.astype(B16), faded[hi])
        ).astype(B16)
        r0 = (mm_tl(tail[lo], x00) + mm_tl(tail[hi], x10)).astype(B16)
        r1 = mm_tl(tail[hi], x11).astype(B16)
        states = mm(r0, pair[lo]) + mm(r1, pair[hi])
        a, b = places(width, width)
        transit = jnp.where(a == b, jnp.exp(end), 0.0) - states[:, width:]
        own[head, 0] = transit
        own[head, 1] = states[:, :width]
        send[0, head, 0] = transit.astype(B16)
        send[0, head, 1] = states[:, :width].astype(B16)
        copy(0, head).start()

    for r in range(rounds):
        head = step - 1 - r

        @pl.when((head >= 0) & (head < heads))
        def _():
            copy(r, head).wait_recv()
            upper = partner(r)[1] == 1
            got_t, got_e = recv[r, head, 0], recv[r, head, 1]
            if r == 0:
                a, b = places(width, width)
                far_state = got_e.astype(F32)
                moved = got_t.astype(F32)
                kept = jnp.where(a == b, 1.0, 0.0)
            else:
                kept = carry[head]
                both = mm(kept.astype(B16), jnp.concatenate([got_t, got_e], -1))
                moved, far_state = both[:, :width], both[:, width:]
            cross[head, :, r * width : (r + 1) * width] = jnp.where(
                upper, far_state, 0.0
            ).astype(B16)
            if r < rounds - 1:
                carry[head] = jnp.where(upper, moved, kept)
                mine_t, mine_e = own[head, 0], own[head, 1]
                left = jnp.where(upper, mine_t, got_t.astype(F32)).astype(B16)
                right_t = jnp.where(upper, got_t.astype(F32), mine_t).astype(B16)
                right_e = jnp.where(upper, got_e.astype(F32), mine_e).astype(B16)
                later = jnp.where(upper, mine_e, got_e.astype(F32))
                joined = mm(left, jnp.concatenate([right_t, right_e], -1))
                new_t = joined[:, :width]
                new_e = joined[:, width:] + later
                own[head, 0] = new_t
                own[head, 1] = new_e
                send[r + 1, head, 0] = new_t.astype(B16)
                send[r + 1, head, 1] = new_e.astype(B16)
                copy(r + 1, head).start()

    @pl.when(step >= rounds)
    def _():
        head = step - rounds
        for r in range(rounds):
            rows[2 + r : 3 + r, :] = weight_ref[1 + depth + r, pl.ds(head, 1), :]
        cols = rows[...].T
        far = mm(seen[head], cross[head])
        total = local[head]
        for r in range(rounds):
            total = total + cols[:, 2 + r : 3 + r] * far[:, r * width : (r + 1) * width]
        scaled = total * lax.rsqrt(jnp.mean(total * total, -1, keepdims=True) + 1e-06)
        o_ref[...] = (scaled * gain_ref[...]).astype(B16)

        for r in range(rounds):
            copy(r, head).wait_send()


def attention(query, keys, values, log_decay, beta, level_weights, norm_gain):
    tokens = query.shape[0]
    heads = log_decay.shape[0]
    width = query.shape[1] // heads
    levels = level_weights.shape[0]
    rounds = lax.axis_size("seq").bit_length() - 1
    depth = levels - 1 - rounds

    def head_in(i):
        return (0, jnp.minimum(i, heads - 1))

    def head_out(i):
        return (0, jnp.maximum(i - rounds, 0))

    token_block = pl.BlockSpec((tokens, width), head_in)
    whole2 = pl.BlockSpec((heads, tokens), lambda i: (0, 0))
    return pl.pallas_call(
        functools.partial(attention_kernel, heads, rounds, depth),
        grid=(heads + rounds,),
        out_shape=jax.ShapeDtypeStruct((tokens, heads * width), B16),
        in_specs=[
            token_block, token_block, token_block, whole2, whole2,
            pl.BlockSpec((levels, heads, tokens), lambda i: (0, 0, 0)),
            pl.BlockSpec((1, width), head_out),
        ],
        out_specs=pl.BlockSpec((tokens, width), head_out),
        scratch_shapes=[
            pltpu.VMEM((heads, tokens), F32),
            pltpu.VMEM((16, tokens), F32),
            pltpu.VMEM((heads, tokens, width), F32),
            pltpu.VMEM((heads, tokens, width), B16),
            pltpu.VMEM((heads, 2, width, width), F32),
            pltpu.VMEM((heads, width, width), F32),
            pltpu.VMEM((heads, width, rounds * width), B16),
            pltpu.VMEM((rounds, heads, 2, width, width), B16),
            pltpu.VMEM((rounds, heads, 2, width, width), B16),
            pltpu.SemaphoreType.DMA((rounds, heads)),
            pltpu.SemaphoreType.DMA((rounds, heads)),
        ],
        compiler_params=pltpu.CompilerParams(
            collective_id=0, has_side_effects=True, vmem_limit_bytes=48 << 20
        ),
    )(query, keys, values, log_decay, beta, level_weights, norm_gain.reshape(1, -1))


def per_device(query, keys, values, log_decay, beta, level_weights, norm_gain, out_weight):
    normed = attention(query, keys, values, log_decay, beta, level_weights, norm_gain)
    return lax.psum_scatter(
        jnp.dot(normed, out_weight, preferred_element_type=F32).astype(B16),
        "head",
        scatter_dimension=0,
        tiled=True,
    )


def solution(mesh):
    placed = (
        P("seq", "head"),
        P("seq", "head"),
        P("seq", "head"),
        P("head", "seq"),
        P("head", "seq"),
        P(None, "head", "seq"),
        P("head"),
        P("head", None),
    )
    return jax.shard_map(
        per_device, mesh=mesh, in_specs=placed, out_specs=P(("seq", "head"), None), check_vma=False
    )
```

```python
import functools

import jax
import jax.numpy as jnp
from jax import lax
from jax.experimental import pallas as pl
from jax.experimental.pallas import tpu as pltpu
from jax.sharding import PartitionSpec as P

BLK = 64
HALF = 256
MESH = pl.DeviceIdType.MESH
F32 = jnp.float32
B16 = jnp.bfloat16


def mm(left, right):
    return jnp.dot(left, right, preferred_element_type=F32)


def mm_t(left, right):
    return lax.dot_general(left, right, (((1,), (1,)), ((), ())), preferred_element_type=F32)


def mm_tl(left, right):
    return lax.dot_general(left, right, (((0,), (0,)), ((), ())), preferred_element_type=F32)


def unit_rows(matrix):
    return matrix * lax.rsqrt(jnp.sum(matrix * matrix, -1, keepdims=True) + 1e-06)


def places(rows, cols):
    return (
        lax.broadcasted_iota(jnp.int32, (rows, cols), 0),
        lax.broadcasted_iota(jnp.int32, (rows, cols), 1),
    )


def unit_lower_inverses(lowers):
    row, col = places(HALF, HALF)
    apart = row ^ col
    eye = jnp.where(row == col, 1.0, 0.0)
    ys = [jnp.where(apart < 16, -low, 0.0) for low in lowers]
    yb = [y.astype(B16) for y in ys]
    y2 = [mm(y, y) for y in yb]
    y2b = [y.astype(B16) for y in y2]
    y3 = [mm(y, z) for y, z in zip(yb, y2b)]
    y4b = [mm(y, y).astype(B16) for y in y2b]
    first = [eye + a + b + c for a, b, c in zip(ys, y2, y3)]
    y8b = [mm(y, y).astype(B16) for y in y4b]
    second = [a + mm(a.astype(B16), y) for a, y in zip(first, y4b)]
    xs = [a + mm(a.astype(B16), y) for a, y in zip(second, y8b)]
    size = 16
    while size < HALF:
        ring = (apart >= size) & (apart < 2 * size)
        xb = [x.astype(B16) for x in xs]
        inner = [
            mm(jnp.where(ring, low, 0.0).astype(B16), x).astype(B16) for low, x in zip(lowers, xb)
        ]
        xs = [x - mm(b, t) for x, b, t in zip(xs, xb, inner)]
        size *= 2
    return [x.astype(B16) for x in xs]


def attention_kernel(
    heads, group, rounds, depth,
    q_ref, k_ref, v_ref, decay_ref, beta_ref, weight_ref, gain_ref,
    o_ref,
    running, rows, local, seen, own, carry, cross, send, recv, send_sem, recv_sem,
):
    step = pl.program_id(0)
    me = lax.axis_index("seq")
    tokens = q_ref.shape[0]
    width = q_ref.shape[1] // group
    groups = heads // group

    def partner(r):
        bit = (me // (1 << r)) % 2
        return me + (1 - 2 * bit) * (1 << r), bit

    def copy(r, part):
        first = 1 if r == rounds - 1 else 0
        return pltpu.make_async_remote_copy(
            src_ref=send.at[r, part, pl.ds(first, 2 - first)],
            dst_ref=recv.at[r, part, pl.ds(first, 2 - first)],
            send_sem=send_sem.at[r, part],
            recv_sem=recv_sem.at[r, part],
            device_id={"seq": partner(r)[0]},
            device_id_type=MESH,
        )

    @pl.when(step == 0)
    def _():
        barrier = pltpu.get_barrier_semaphore()
        for r in range(rounds):
            pl.semaphore_signal(
                barrier, inc=1, device_id={"seq": partner(r)[0]}, device_id_type=MESH
            )
        pl.semaphore_wait(barrier, rounds)
        total = decay_ref[...]
        lane = lax.broadcasted_iota(jnp.int32, total.shape, 1)
        shift = 1
        while shift < tokens:
            total = total + jnp.where(lane >= shift, pltpu.roll(total, shift, 1), 0.0)
            shift *= 2
        running[...] = total
        rows[...] = jnp.zeros_like(rows)

    @pl.when(step < groups)
    def _():
        part = step
        row, col = places(HALF, HALF)
        apart = row ^ col
        on_below = row >= col
        below = row > col
        lo, hi = slice(0, HALF), slice(HALF, 2 * HALF)
        work = []
        for u in range(group):
            head = part * group + u
            rows[u, 0:1, :] = running[pl.ds(head, 1), :]
            rows[u, 1:2, :] = beta_ref[pl.ds(head, 1), :]
            for level in range(1 + depth):
                rows[u, 2 + level : 3 + level, :] = weight_ref[level, pl.ds(head, 1), :]
            run_row = rows[u, 0:1, :]
            cols = rows[u].T
            run = cols[:, 0:1]
            beta = cols[:, 1:2]
            gamma = jnp.exp(run)
            end = run[tokens - 1 : tokens, :]
            lanes = slice(u * width, (u + 1) * width)
            qn = unit_rows(q_ref[:, lanes].astype(F32))
            kn = unit_rows(k_ref[:, lanes].astype(F32))
            qb = qn.astype(B16)
            kb = kn.astype(B16)
            fresh = (beta * v_ref[:, lanes].astype(F32)).astype(B16)
            faded = (beta * gamma * kn).astype(B16)
            pair = jnp.concatenate([fresh, faded], -1)
            tail = (jnp.exp(end - run) * kn).astype(B16)

            def decay(i, j):
                gap = jnp.exp(jnp.minimum(run[i] - run_row[:, j], 0.0))
                return jnp.where(on_below, gap, 0.0) if i == j else gap

            d00, d10, d11 = decay(lo, lo), decay(hi, lo), decay(hi, hi)
            l00 = jnp.where(below, beta[lo] * d00 * mm_t(kb[lo], kb[lo]), 0.0)
            l11 = jnp.where(below, beta[hi] * d11 * mm_t(kb[hi], kb[hi]), 0.0)
            l10 = (beta[hi] * d10 * mm_t(kb[hi], kb[lo])).astype(B16)
            m00 = (d00 * mm_t(qb[lo], kb[lo])).astype(B16)
            m11 = (d11 * mm_t(qb[hi], kb[hi])).astype(B16)
            m10 = (d10 * mm_t(qb[hi], kb[lo])).astype(B16)
            work.append((cols, gamma, end, qn, fresh, faded, pair, tail, l00, l11, l10, m00, m11, m10))
        inverses = unit_lower_inverses([low for item in work for low in item[8:10]])
        x10s = [
            mm(item[10], inverses[2 * u]).astype(B16) for u, item in enumerate(work)
        ]
        x10s = [(-mm(inverses[2 * u + 1], x)).astype(B16) for u, x in enumerate(x10s)]
        for u, item in enumerate(work):
            head = part * group + u
            cols, gamma, end, qn, fresh, faded, pair, tail, _, _, _, m00, m11, m10 = item
            x00, x11, x10 = inverses[2 * u], inverses[2 * u + 1], x10s[u]
            p00 = mm(m00, x00)
            p11 = mm(m11, x11)
            p10 = (mm(m10, x00) + mm(m11, x10)).astype(B16)

            def level_weight(i):
                chosen = cols[i, 1 + depth : 2 + depth]
                for level in range(depth - 2, -1, -1):
                    chosen = jnp.where(apart < (BLK << level), cols[i, 2 + level : 3 + level], chosen)
                return chosen

            both = mm(p10, pair[lo])
            local[head, lo, :] = mm((level_weight(lo) * p00).astype(B16), fresh[lo])
            local[head, hi, :] = (
                mm((level_weight(hi) * p11).astype(B16), fresh[hi])
                + cols[hi, 2 + depth : 3 + depth] * both[:, :width]
            )
            seen[head, lo, :] = (gamma[lo] * qn[lo] - mm(p00.astype(B16), faded[lo])).astype(B16)
            seen[head, hi, :] = (
                gamma[hi] * qn[hi] - both[:, width:] - mm(p11.astype(B16), faded[hi])
            ).astype(B16)
            r0 = (mm_tl(tail[lo], x00) + mm_tl(tail[hi], x10)).astype(B16)
            r1 = mm_tl(tail[hi], x11).astype(B16)
            states = mm(r0, pair[lo]) + mm(r1, pair[hi])
            a, b = places(width, width)
            transit = jnp.where(a == b, jnp.exp(end), 0.0) - states[:, width:]
            own[head, 0] = transit
            own[head, 1] = states[:, :width]
            send[0, part, 0, u] = transit.astype(B16)
            send[0, part, 1, u] = states[:, :width].astype(B16)
        copy(0, part).start()

    for r in range(rounds):
        part = step - 1 - r

        @pl.when((part >= 0) & (part < groups))
        def _():
            copy(r, part).wait_recv()
            upper = partner(r)[1] == 1
            for u in range(group):
                head = part * group + u
                got_e = recv[r, part, 1, u]
                if r == rounds - 1:
                    kept = carry[head] if r > 0 else None
                    far_state = mm(kept.astype(B16), got_e) if r > 0 else got_e.astype(F32)
                    cross[head, :, r * width : (r + 1) * width] = jnp.where(
                        upper, far_state, 0.0
                    ).astype(B16)
                    continue
                got_t = recv[r, part, 0, u]
                if r == 0:
                    a, b = places(width, width)
                    far_state = got_e.astype(F32)
                    moved = got_t.astype(F32)
                    kept = jnp.where(a == b, 1.0, 0.0)
                else:
                    kept = carry[head]
                    both = mm(kept.astype(B16), jnp.concatenate([got_t, got_e], -1))
                    moved, far_state = both[:, :width], both[:, width:]
                cross[head, :, r * width : (r + 1) * width] = jnp.where(
                    upper, far_state, 0.0
                ).astype(B16)
                carry[head] = jnp.where(upper, moved, kept)
                mine_t, mine_e = own[head, 0], own[head, 1]
                left = jnp.where(upper, mine_t, got_t.astype(F32)).astype(B16)
                right_t = jnp.where(upper, got_t.astype(F32), mine_t).astype(B16)
                right_e = jnp.where(upper, got_e.astype(F32), mine_e).astype(B16)
                later = jnp.where(upper, mine_e, got_e.astype(F32))
                joined = mm(left, jnp.concatenate([right_t, right_e], -1))
                new_t = joined[:, :width]
                new_e = joined[:, width:] + later
                own[head, 0] = new_t
                own[head, 1] = new_e
                send[r + 1, part, 0, u] = new_t.astype(B16)
                send[r + 1, part, 1, u] = new_e.astype(B16)
            if r < rounds - 1:
                copy(r + 1, part).start()

    @pl.when(step >= rounds)
    def _():
        part = step - rounds
        for u in range(group):
            head = part * group + u
            lanes = slice(u * width, (u + 1) * width)
            for r in range(rounds):
                rows[u, 2 + r : 3 + r, :] = weight_ref[1 + depth + r, pl.ds(head, 1), :]
            cols = rows[u].T
            far = mm(seen[head], cross[head])
            total = local[head]
            for r in range(rounds):
                total = total + cols[:, 2 + r : 3 + r] * far[:, r * width : (r + 1) * width]
            scaled = total * lax.rsqrt(jnp.mean(total * total, -1, keepdims=True) + 1e-06)
            o_ref[:, lanes] = (scaled * gain_ref[:, lanes]).astype(B16)

        for r in range(rounds):
            copy(r, part).wait_send()


def attention(query, keys, values, log_decay, beta, level_weights, norm_gain):
    tokens = query.shape[0]
    heads = log_decay.shape[0]
    width = query.shape[1] // heads
    levels = level_weights.shape[0]
    rounds = lax.axis_size("seq").bit_length() - 1
    depth = levels - 1 - rounds
    group = 2
    groups = heads // group

    def head_in(i):
        return (0, jnp.minimum(i, groups - 1))

    def head_out(i):
        return (0, jnp.maximum(i - rounds, 0))

    token_block = pl.BlockSpec((tokens, group * width), head_in)
    whole2 = pl.BlockSpec((heads, tokens), lambda i: (0, 0))
    return pl.pallas_call(
        functools.partial(attention_kernel, heads, group, rounds, depth),
        grid=(groups + rounds,),
        out_shape=jax.ShapeDtypeStruct((tokens, heads * width), B16),
        in_specs=[
            token_block, token_block, token_block, whole2, whole2,
            pl.BlockSpec((levels, heads, tokens), lambda i: (0, 0, 0)),
            pl.BlockSpec((1, group * width), head_out),
        ],
        out_specs=pl.BlockSpec((tokens, group * width), head_out),
        scratch_shapes=[
            pltpu.VMEM((heads, tokens), F32),
            pltpu.VMEM((group, 16, tokens), F32),
            pltpu.VMEM((heads, tokens, width), F32),
            pltpu.VMEM((heads, tokens, width), B16),
            pltpu.VMEM((heads, 2, width, width), F32),
            pltpu.VMEM((heads, width, width), F32),
            pltpu.VMEM((heads, width, rounds * width), B16),
            pltpu.VMEM((rounds, groups, 2, group, width, width), B16),
            pltpu.VMEM((rounds, groups, 2, group, width, width), B16),
            pltpu.SemaphoreType.DMA((rounds, groups)),
            pltpu.SemaphoreType.DMA((rounds, groups)),
        ],
        compiler_params=pltpu.CompilerParams(
            collective_id=0, has_side_effects=True, vmem_limit_bytes=60 << 20
        ),
    )(query, keys, values, log_decay, beta, level_weights, norm_gain.reshape(1, -1))


def project_kernel(
    span, chunks, n_ref, w_ref, o_ref, parts, send, recv, send_sem, recv_sem
):
    step = pl.program_id(0)
    me = lax.axis_index("head")
    rows = o_ref.shape[0]
    has_left, has_right = me > 0, me < span - 1

    def rightward(dest, chunk):
        return pltpu.make_async_remote_copy(
            src_ref=send.at[dest, chunk],
            dst_ref=recv.at[dest, chunk],
            send_sem=send_sem.at[dest, chunk],
            recv_sem=recv_sem.at[dest, chunk],
            device_id={"head": me + 1},
            device_id_type=MESH,
        )

    def leftward(dest, chunk, slot):
        return pltpu.make_async_remote_copy(
            src_ref=send.at[dest, chunk],
            dst_ref=recv.at[slot, chunk],
            send_sem=send_sem.at[dest, chunk],
            recv_sem=recv_sem.at[slot, chunk],
            device_id={"head": me - 1},
            device_id_type=MESH,
        )

    def leftward_slot(dest):
        return jnp.where(dest == me - 1, span, dest)

    @pl.when(step == 0)
    def _():
        barrier = pltpu.get_barrier_semaphore()

        @pl.when(has_left)
        def _():
            pl.semaphore_signal(barrier, inc=1, device_id={"head": me - 1}, device_id_type=MESH)

        @pl.when(has_right)
        def _():
            pl.semaphore_signal(barrier, inc=1, device_id={"head": me + 1}, device_id_type=MESH)

        neighbours = jnp.where(has_left, 1, 0) + jnp.where(has_right, 1, 0)
        pl.semaphore_wait(barrier, neighbours)

    @pl.when(step < chunks)
    def _():
        chunk = step
        parts[chunk] = mm(n_ref[...], w_ref[...])

        for dest in range(span - 1, 0, -1):
            @pl.when(me == 0)
            def _():
                send[dest, chunk] = parts[chunk, dest * rows : (dest + 1) * rows, :].astype(B16)
                rightward(dest, chunk).start()

        for dest in range(span - 1):
            @pl.when(me == span - 1)
            def _():
                send[dest, chunk] = parts[chunk, dest * rows : (dest + 1) * rows, :].astype(B16)
                leftward(dest, chunk, leftward_slot(dest)).start()

    @pl.when(step >= chunks)
    def _():
        chunk = step - chunks

        for far in range(span - 1):
            right_dest, left_dest = span - 1 - far, far

            @pl.when(has_left & (right_dest > me))
            def _():
                rightward(right_dest, chunk).wait_recv()
                send[right_dest, chunk] = (
                    parts[chunk, right_dest * rows : (right_dest + 1) * rows, :]
                    + recv[right_dest, chunk].astype(F32)
                ).astype(B16)
                rightward(right_dest, chunk).start()

            @pl.when(has_right & (left_dest < me))
            def _():
                leftward(left_dest, chunk, left_dest).wait_recv()
                send[left_dest, chunk] = (
                    parts[chunk, left_dest * rows : (left_dest + 1) * rows, :]
                    + recv[left_dest, chunk].astype(F32)
                ).astype(B16)
                leftward(left_dest, chunk, leftward_slot(left_dest)).start()

        for dest in range(span):
            @pl.when(dest == me)
            def _():
                mine = parts[chunk, dest * rows : (dest + 1) * rows, :]
                if dest > 0:
                    rightward(dest, chunk).wait_recv()
                    mine = mine + recv[dest, chunk].astype(F32)
                if dest < span - 1:
                    leftward(dest, chunk, span).wait_recv()
                    mine = mine + recv[span, chunk].astype(F32)
                o_ref[...] = mine.astype(B16)

    @pl.when(step == 2 * chunks - 1)
    def _():
        @pl.loop(0, chunks)
        def _(chunk):
            for dest in range(span):
                @pl.when(dest > me)
                def _():
                    rightward(dest, chunk).wait_send()

                @pl.when(dest < me)
                def _():
                    leftward(dest, chunk, leftward_slot(dest)).wait_send()


def project(normed, out_weight):
    tokens, inner = normed.shape
    columns = out_weight.shape[1]
    span = lax.axis_size("head")
    rows = tokens // span
    piece = 512
    chunks = columns // piece
    return pl.pallas_call(
        functools.partial(project_kernel, span, chunks),
        grid=(2 * chunks,),
        out_shape=jax.ShapeDtypeStruct((rows, columns), B16),
        in_specs=[
            pl.BlockSpec((tokens, inner), lambda i: (0, 0)),
            pl.BlockSpec((inner, piece), lambda i: (0, jnp.minimum(i, chunks - 1))),
        ],
        out_specs=pl.BlockSpec((rows, piece), lambda i: (0, jnp.maximum(i - chunks, 0))),
        scratch_shapes=[
            pltpu.VMEM((chunks, tokens, piece), F32),
            pltpu.VMEM((span, chunks, rows, piece), B16),
            pltpu.VMEM((span + 1, chunks, rows, piece), B16),
            pltpu.SemaphoreType.DMA((span, chunks)),
            pltpu.SemaphoreType.DMA((span + 1, chunks)),
        ],
        compiler_params=pltpu.CompilerParams(
            collective_id=1, has_side_effects=True, vmem_limit_bytes=60 << 20
        ),
    )(normed, out_weight)


def per_device(query, keys, values, log_decay, beta, level_weights, norm_gain, out_weight):
    normed = attention(query, keys, values, log_decay, beta, level_weights, norm_gain)
    return project(normed, out_weight)


def solution(mesh):
    placed = (
        P("seq", "head"),
        P("seq", "head"),
        P("seq", "head"),
        P("head", "seq"),
        P("head", "seq"),
        P(None, "head", "seq"),
        P("head"),
        P("head", None),
    )
    return jax.shard_map(
        per_device, mesh=mesh, in_specs=placed, out_specs=P(("seq", "head"), None), check_vma=False
    )
```

```python
import functools

import jax
import jax.numpy as jnp
from jax import lax
from jax.experimental import pallas as pl
from jax.experimental.pallas import tpu as pltpu
from jax.sharding import PartitionSpec as P

BLK = 64
HALF = 256
MESH = pl.DeviceIdType.MESH
F32 = jnp.float32
B16 = jnp.bfloat16


def mm(left, right):
    return jnp.dot(left, right, preferred_element_type=F32)


def mm_t(left, right):
    return lax.dot_general(left, right, (((1,), (1,)), ((), ())), preferred_element_type=F32)


def mm_tl(left, right):
    return lax.dot_general(left, right, (((0,), (0,)), ((), ())), preferred_element_type=F32)


def unit_rows(matrix):
    return matrix * lax.rsqrt(jnp.sum(matrix * matrix, -1, keepdims=True) + 1e-06)


def places(rows, cols):
    return (
        lax.broadcasted_iota(jnp.int32, (rows, cols), 0),
        lax.broadcasted_iota(jnp.int32, (rows, cols), 1),
    )


def unit_lower_inverses(lowers):
    row, col = places(HALF, HALF)
    apart = row ^ col
    eye = jnp.where(row == col, 1.0, 0.0)
    ys = [jnp.where(apart < 16, -low, 0.0) for low in lowers]
    yb = [y.astype(B16) for y in ys]
    y2 = [mm(y, y) for y in yb]
    y2b = [y.astype(B16) for y in y2]
    y3 = [mm(y, z) for y, z in zip(yb, y2b)]
    y4b = [mm(y, y).astype(B16) for y in y2b]
    first = [eye + a + b + c for a, b, c in zip(ys, y2, y3)]
    y8b = [mm(y, y).astype(B16) for y in y4b]
    second = [a + mm(a.astype(B16), y) for a, y in zip(first, y4b)]
    xs = [a + mm(a.astype(B16), y) for a, y in zip(second, y8b)]
    size = 16
    while size < HALF:
        ring = (apart >= size) & (apart < 2 * size)
        xb = [x.astype(B16) for x in xs]
        inner = [
            mm(jnp.where(ring, low, 0.0).astype(B16), x).astype(B16) for low, x in zip(lowers, xb)
        ]
        xs = [x - mm(b, t) for x, b, t in zip(xs, xb, inner)]
        size *= 2
    return [x.astype(B16) for x in xs]


def attention_kernel(
    heads, group, rounds, depth,
    q_ref, k_ref, v_ref, decay_ref, beta_ref, weight_ref, gain_ref,
    o_ref,
    running, rows, local, seen, own, carry, cross, send, recv, send_sem, recv_sem,
):
    step = pl.program_id(0)
    me = lax.axis_index("seq")
    tokens = q_ref.shape[0]
    width = q_ref.shape[1] // group
    groups = heads // group

    def partner(r):
        bit = (me // (1 << r)) % 2
        return me + (1 - 2 * bit) * (1 << r), bit

    def copy(r, part):
        first = 1 if r == rounds - 1 else 0
        return pltpu.make_async_remote_copy(
            src_ref=send.at[r, part, pl.ds(first, 2 - first)],
            dst_ref=recv.at[r, part, pl.ds(first, 2 - first)],
            send_sem=send_sem.at[r, part],
            recv_sem=recv_sem.at[r, part],
            device_id={"seq": partner(r)[0]},
            device_id_type=MESH,
        )

    @pl.when(step == 0)
    def _():
        barrier = pltpu.get_barrier_semaphore()
        for r in range(rounds):
            pl.semaphore_signal(
                barrier, inc=1, device_id={"seq": partner(r)[0]}, device_id_type=MESH
            )
        pl.semaphore_wait(barrier, rounds)
        total = decay_ref[...]
        lane = lax.broadcasted_iota(jnp.int32, total.shape, 1)
        shift = 1
        while shift < tokens:
            total = total + jnp.where(lane >= shift, pltpu.roll(total, shift, 1), 0.0)
            shift *= 2
        running[...] = total
        rows[...] = jnp.zeros_like(rows)

    @pl.when(step < groups)
    def _():
        part = step
        row, col = places(HALF, HALF)
        apart = row ^ col
        on_below = row >= col
        below = row > col
        lo, hi = slice(0, HALF), slice(HALF, 2 * HALF)
        work = []
        for u in range(group):
            head = part * group + u
            rows[u, 0:1, :] = running[pl.ds(head, 1), :]
            rows[u, 1:2, :] = beta_ref[pl.ds(head, 1), :]
            for level in range(1 + depth):
                rows[u, 2 + level : 3 + level, :] = weight_ref[level, pl.ds(head, 1), :]
            run_row = rows[u, 0:1, :]
            cols = rows[u].T
            run = cols[:, 0:1]
            beta = cols[:, 1:2]
            gamma = jnp.exp(run)
            end = run[tokens - 1 : tokens, :]
            lanes = slice(u * width, (u + 1) * width)
            qn = unit_rows(q_ref[:, lanes].astype(F32))
            kn = unit_rows(k_ref[:, lanes].astype(F32))
            qb = qn.astype(B16)
            kb = kn.astype(B16)
            fresh = (beta * v_ref[:, lanes].astype(F32)).astype(B16)
            faded = (beta * gamma * kn).astype(B16)
            pair = jnp.concatenate([fresh, faded], -1)
            tail = (jnp.exp(end - run) * kn).astype(B16)

            def decay(i, j):
                gap = jnp.exp(jnp.minimum(run[i] - run_row[:, j], 0.0))
                return jnp.where(on_below, gap, 0.0) if i == j else gap

            d00, d10, d11 = decay(lo, lo), decay(hi, lo), decay(hi, hi)
            l00 = jnp.where(below, beta[lo] * d00 * mm_t(kb[lo], kb[lo]), 0.0)
            l11 = jnp.where(below, beta[hi] * d11 * mm_t(kb[hi], kb[hi]), 0.0)
            l10 = (beta[hi] * d10 * mm_t(kb[hi], kb[lo])).astype(B16)
            m00 = (d00 * mm_t(qb[lo], kb[lo])).astype(B16)
            m11 = (d11 * mm_t(qb[hi], kb[hi])).astype(B16)
            m10 = (d10 * mm_t(qb[hi], kb[lo])).astype(B16)
            work.append((cols, gamma, end, qn, fresh, faded, pair, tail, l00, l11, l10, m00, m11, m10))
        inverses = unit_lower_inverses([low for item in work for low in item[8:10]])
        x10s = [
            mm(item[10], inverses[2 * u]).astype(B16) for u, item in enumerate(work)
        ]
        x10s = [(-mm(inverses[2 * u + 1], x)).astype(B16) for u, x in enumerate(x10s)]
        for u, item in enumerate(work):
            head = part * group + u
            cols, gamma, end, qn, fresh, faded, pair, tail, _, _, _, m00, m11, m10 = item
            x00, x11, x10 = inverses[2 * u], inverses[2 * u + 1], x10s[u]
            p00 = mm(m00, x00)
            p11 = mm(m11, x11)
            p10 = (mm(m10, x00) + mm(m11, x10)).astype(B16)

            def level_weight(i):
                chosen = cols[i, 1 + depth : 2 + depth]
                for level in range(depth - 2, -1, -1):
                    chosen = jnp.where(apart < (BLK << level), cols[i, 2 + level : 3 + level], chosen)
                return chosen

            both = mm(p10, pair[lo])
            local[head, lo, :] = mm((level_weight(lo) * p00).astype(B16), fresh[lo])
            local[head, hi, :] = (
                mm((level_weight(hi) * p11).astype(B16), fresh[hi])
                + cols[hi, 2 + depth : 3 + depth] * both[:, :width]
            )
            seen[head, lo, :] = (gamma[lo] * qn[lo] - mm(p00.astype(B16), faded[lo])).astype(B16)
            seen[head, hi, :] = (
                gamma[hi] * qn[hi] - both[:, width:] - mm(p11.astype(B16), faded[hi])
            ).astype(B16)
            r0 = (mm_tl(tail[lo], x00) + mm_tl(tail[hi], x10)).astype(B16)
            r1 = mm_tl(tail[hi], x11).astype(B16)
            states = mm(r0, pair[lo]) + mm(r1, pair[hi])
            a, b = places(width, width)
            transit = jnp.where(a == b, jnp.exp(end), 0.0) - states[:, width:]
            own[head, 0] = transit
            own[head, 1] = states[:, :width]
            send[0, part, 0, u] = transit.astype(B16)
            send[0, part, 1, u] = states[:, :width].astype(B16)
        copy(0, part).start()

    for r in range(rounds):
        part = step - 1 - r

        @pl.when((part >= 0) & (part < groups))
        def _():
            copy(r, part).wait_recv()
            upper = partner(r)[1] == 1
            for u in range(group):
                head = part * group + u
                got_e = recv[r, part, 1, u]
                if r == rounds - 1:
                    kept = carry[head] if r > 0 else None
                    far_state = mm(kept.astype(B16), got_e) if r > 0 else got_e.astype(F32)
                    cross[head, :, r * width : (r + 1) * width] = jnp.where(
                        upper, far_state, 0.0
                    ).astype(B16)
                    continue
                got_t = recv[r, part, 0, u]
                if r == 0:
                    a, b = places(width, width)
                    far_state = got_e.astype(F32)
                    moved = got_t.astype(F32)
                    kept = jnp.where(a == b, 1.0, 0.0)
                else:
                    kept = carry[head]
                    both = mm(kept.astype(B16), jnp.concatenate([got_t, got_e], -1))
                    moved, far_state = both[:, :width], both[:, width:]
                cross[head, :, r * width : (r + 1) * width] = jnp.where(
                    upper, far_state, 0.0
                ).astype(B16)
                carry[head] = jnp.where(upper, moved, kept)
                mine_t, mine_e = own[head, 0], own[head, 1]
                left = jnp.where(upper, mine_t, got_t.astype(F32)).astype(B16)
                right_t = jnp.where(upper, got_t.astype(F32), mine_t).astype(B16)
                right_e = jnp.where(upper, got_e.astype(F32), mine_e).astype(B16)
                later = jnp.where(upper, mine_e, got_e.astype(F32))
                joined = mm(left, jnp.concatenate([right_t, right_e], -1))
                new_t = joined[:, :width]
                new_e = joined[:, width:] + later
                own[head, 0] = new_t
                own[head, 1] = new_e
                send[r + 1, part, 0, u] = new_t.astype(B16)
                send[r + 1, part, 1, u] = new_e.astype(B16)
            if r < rounds - 1:
                copy(r + 1, part).start()

    @pl.when(step >= rounds)
    def _():
        part = step - rounds
        for u in range(group):
            head = part * group + u
            lanes = slice(u * width, (u + 1) * width)
            for r in range(rounds):
                rows[u, 2 + r : 3 + r, :] = weight_ref[1 + depth + r, pl.ds(head, 1), :]
            cols = rows[u].T
            far = mm(seen[head], cross[head])
            total = local[head]
            for r in range(rounds):
                total = total + cols[:, 2 + r : 3 + r] * far[:, r * width : (r + 1) * width]
            scaled = total * lax.rsqrt(jnp.mean(total * total, -1, keepdims=True) + 1e-06)
            o_ref[:, lanes] = (scaled * gain_ref[:, lanes]).astype(B16)

        for r in range(rounds):
            copy(r, part).wait_send()


def attention(query, keys, values, log_decay, beta, level_weights, norm_gain):
    tokens = query.shape[0]
    heads = log_decay.shape[0]
    width = query.shape[1] // heads
    levels = level_weights.shape[0]
    rounds = lax.axis_size("seq").bit_length() - 1
    depth = levels - 1 - rounds
    group = 2
    groups = heads // group

    def head_in(i):
        return (0, jnp.minimum(i, groups - 1))

    def head_out(i):
        return (0, jnp.maximum(i - rounds, 0))

    token_block = pl.BlockSpec((tokens, group * width), head_in)
    whole2 = pl.BlockSpec((heads, tokens), lambda i: (0, 0))
    return pl.pallas_call(
        functools.partial(attention_kernel, heads, group, rounds, depth),
        grid=(groups + rounds,),
        out_shape=jax.ShapeDtypeStruct((tokens, heads * width), B16),
        in_specs=[
            token_block, token_block, token_block, whole2, whole2,
            pl.BlockSpec((levels, heads, tokens), lambda i: (0, 0, 0)),
            pl.BlockSpec((1, group * width), head_out),
        ],
        out_specs=pl.BlockSpec((tokens, group * width), head_out),
        scratch_shapes=[
            pltpu.VMEM((heads, tokens), F32),
            pltpu.VMEM((group, 16, tokens), F32),
            pltpu.VMEM((heads, tokens, width), F32),
            pltpu.VMEM((heads, tokens, width), B16),
            pltpu.VMEM((heads, 2, width, width), F32),
            pltpu.VMEM((heads, width, width), F32),
            pltpu.VMEM((heads, width, rounds * width), B16),
            pltpu.VMEM((rounds, groups, 2, group, width, width), B16),
            pltpu.VMEM((rounds, groups, 2, group, width, width), B16),
            pltpu.SemaphoreType.DMA((rounds, groups)),
            pltpu.SemaphoreType.DMA((rounds, groups)),
        ],
        compiler_params=pltpu.CompilerParams(
            collective_id=0, has_side_effects=True, vmem_limit_bytes=60 << 20
        ),
    )(query, keys, values, log_decay, beta, level_weights, norm_gain.reshape(1, -1))


def project(normed, weight):
    shares = jnp.dot(normed, weight, preferred_element_type=F32).astype(B16)
    return lax.psum_scatter(shares, "head", scatter_dimension=0, tiled=True)


def per_device(query, keys, values, log_decay, beta, level_weights, norm_gain, out_weight):
    normed = attention(query, keys, values, log_decay, beta, level_weights, norm_gain)
    cut = out_weight.shape[1] // 4
    return jnp.concatenate(
        [project(normed, out_weight[:, :cut]), project(normed, out_weight[:, cut:])], -1
    )


def solution(mesh):
    placed = (
        P("seq", "head"),
        P("seq", "head"),
        P("seq", "head"),
        P("head", "seq"),
        P("head", "seq"),
        P(None, "head", "seq"),
        P("head"),
        P("head", None),
    )
    return jax.shard_map(
        per_device, mesh=mesh, in_specs=placed, out_specs=P(("seq", "head"), None), check_vma=False
    )
```

```python
import functools

import jax
import jax.numpy as jnp
from jax import lax
from jax.experimental import pallas as pl
from jax.experimental.pallas import tpu as pltpu
from jax.sharding import PartitionSpec as P

BLK = 64
HALF = 256
MESH = pl.DeviceIdType.MESH
F32 = jnp.float32
B16 = jnp.bfloat16


def mm(left, right):
    return jnp.dot(left, right, preferred_element_type=F32)


def mm_t(left, right):
    return lax.dot_general(left, right, (((1,), (1,)), ((), ())), preferred_element_type=F32)


def mm_tl(left, right):
    return lax.dot_general(left, right, (((0,), (0,)), ((), ())), preferred_element_type=F32)


def unit_rows(matrix):
    return matrix * lax.rsqrt(jnp.sum(matrix * matrix, -1, keepdims=True) + 1e-06)


def places(rows, cols):
    return (
        lax.broadcasted_iota(jnp.int32, (rows, cols), 0),
        lax.broadcasted_iota(jnp.int32, (rows, cols), 1),
    )


def unit_lower_inverses(lowers):
    row, col = places(HALF, HALF)
    apart = row ^ col
    eye = jnp.where(row == col, 1.0, 0.0)
    ys = [jnp.where(apart < 16, -low, 0.0) for low in lowers]
    yb = [y.astype(B16) for y in ys]
    y2 = [mm(y, y) for y in yb]
    y2b = [y.astype(B16) for y in y2]
    y3 = [mm(y, z) for y, z in zip(yb, y2b)]
    y4b = [mm(y, y).astype(B16) for y in y2b]
    first = [eye + a + b + c for a, b, c in zip(ys, y2, y3)]
    y8b = [mm(y, y).astype(B16) for y in y4b]
    second = [a + mm(a.astype(B16), y) for a, y in zip(first, y4b)]
    xs = [a + mm(a.astype(B16), y) for a, y in zip(second, y8b)]
    size = 16
    while size < HALF:
        ring = (apart >= size) & (apart < 2 * size)
        xb = [x.astype(B16) for x in xs]
        inner = [
            mm(jnp.where(ring, low, 0.0).astype(B16), x).astype(B16) for low, x in zip(lowers, xb)
        ]
        xs = [x - mm(b, t) for x, b, t in zip(xs, xb, inner)]
        size *= 2
    return [x.astype(B16) for x in xs]


def attention_kernel(
    heads, group, rounds, depth,
    q_ref, k_ref, v_ref, decay_ref, beta_ref, weight_ref, gain_ref,
    o_ref,
    running, rows, local, seen, own, carry, cross, send, recv, send_sem, recv_sem,
):
    step = pl.program_id(0)
    me = lax.axis_index("seq")
    tokens = q_ref.shape[0]
    width = q_ref.shape[1] // group
    groups = heads // group

    def partner(r):
        bit = (me // (1 << r)) % 2
        return me + (1 - 2 * bit) * (1 << r), bit

    def copy(r, part):
        first = 1 if r == rounds - 1 else 0
        return pltpu.make_async_remote_copy(
            src_ref=send.at[r, part, pl.ds(first, 2 - first)],
            dst_ref=recv.at[r, part, pl.ds(first, 2 - first)],
            send_sem=send_sem.at[r, part],
            recv_sem=recv_sem.at[r, part],
            device_id={"seq": partner(r)[0]},
            device_id_type=MESH,
        )

    @pl.when(step == 0)
    def _():
        barrier = pltpu.get_barrier_semaphore()
        for r in range(rounds):
            pl.semaphore_signal(
                barrier, inc=1, device_id={"seq": partner(r)[0]}, device_id_type=MESH
            )
        pl.semaphore_wait(barrier, rounds)
        total = decay_ref[...]
        lane = lax.broadcasted_iota(jnp.int32, total.shape, 1)
        shift = 1
        while shift < tokens:
            total = total + jnp.where(lane >= shift, pltpu.roll(total, shift, 1), 0.0)
            shift *= 2
        running[...] = total
        rows[...] = jnp.zeros_like(rows)

    @pl.when(step < groups)
    def _():
        part = step
        row, col = places(HALF, HALF)
        apart = row ^ col
        on_below = row >= col
        below = row > col
        lo, hi = slice(0, HALF), slice(HALF, 2 * HALF)
        work = []
        for u in range(group):
            head = part * group + u
            rows[u, 0:1, :] = running[pl.ds(head, 1), :]
            rows[u, 1:2, :] = beta_ref[pl.ds(head, 1), :]
            for level in range(1 + depth):
                rows[u, 2 + level : 3 + level, :] = weight_ref[level, pl.ds(head, 1), :]
            run_row = rows[u, 0:1, :]
            cols = rows[u].T
            run = cols[:, 0:1]
            beta = cols[:, 1:2]
            gamma = jnp.exp(run)
            end = run[tokens - 1 : tokens, :]
            lanes = slice(u * width, (u + 1) * width)
            qn = unit_rows(q_ref[:, lanes].astype(F32))
            kn = unit_rows(k_ref[:, lanes].astype(F32))
            qb = qn.astype(B16)
            kb = kn.astype(B16)
            fresh = (beta * v_ref[:, lanes].astype(F32)).astype(B16)
            faded = (beta * gamma * kn).astype(B16)
            pair = jnp.concatenate([fresh, faded], -1)
            tail = (jnp.exp(end - run) * kn).astype(B16)

            def decay(i, j):
                gap = jnp.exp(jnp.minimum(run[i] - run_row[:, j], 0.0))
                return jnp.where(on_below, gap, 0.0) if i == j else gap

            d00, d10, d11 = decay(lo, lo), decay(hi, lo), decay(hi, hi)
            l00 = jnp.where(below, beta[lo] * d00 * mm_t(kb[lo], kb[lo]), 0.0)
            l11 = jnp.where(below, beta[hi] * d11 * mm_t(kb[hi], kb[hi]), 0.0)
            l10 = (beta[hi] * d10 * mm_t(kb[hi], kb[lo])).astype(B16)
            m00 = (d00 * mm_t(qb[lo], kb[lo])).astype(B16)
            m11 = (d11 * mm_t(qb[hi], kb[hi])).astype(B16)
            m10 = (d10 * mm_t(qb[hi], kb[lo])).astype(B16)
            work.append((cols, gamma, end, qn, fresh, faded, pair, tail, l00, l11, l10, m00, m11, m10))
        inverses = unit_lower_inverses([low for item in work for low in item[8:10]])
        x10s = [
            mm(item[10], inverses[2 * u]).astype(B16) for u, item in enumerate(work)
        ]
        x10s = [(-mm(inverses[2 * u + 1], x)).astype(B16) for u, x in enumerate(x10s)]
        for u, item in enumerate(work):
            head = part * group + u
            cols, gamma, end, qn, fresh, faded, pair, tail, _, _, _, m00, m11, m10 = item
            x00, x11, x10 = inverses[2 * u], inverses[2 * u + 1], x10s[u]
            p00 = mm(m00, x00)
            p11 = mm(m11, x11)
            p10 = (mm(m10, x00) + mm(m11, x10)).astype(B16)

            def level_weight(i):
                chosen = cols[i, 1 + depth : 2 + depth]
                for level in range(depth - 2, -1, -1):
                    chosen = jnp.where(apart < (BLK << level), cols[i, 2 + level : 3 + level], chosen)
                return chosen

            both = mm(p10, pair[lo])
            local[head, lo, :] = mm((level_weight(lo) * p00).astype(B16), fresh[lo])
            local[head, hi, :] = (
                mm((level_weight(hi) * p11).astype(B16), fresh[hi])
                + cols[hi, 2 + depth : 3 + depth] * both[:, :width]
            )
            seen[head, lo, :] = (gamma[lo] * qn[lo] - mm(p00.astype(B16), faded[lo])).astype(B16)
            seen[head, hi, :] = (
                gamma[hi] * qn[hi] - both[:, width:] - mm(p11.astype(B16), faded[hi])
            ).astype(B16)
            r0 = (mm_tl(tail[lo], x00) + mm_tl(tail[hi], x10)).astype(B16)
            r1 = mm_tl(tail[hi], x11).astype(B16)
            states = mm(r0, pair[lo]) + mm(r1, pair[hi])
            a, b = places(width, width)
            transit = jnp.where(a == b, jnp.exp(end), 0.0) - states[:, width:]
            own[head, 0] = transit
            own[head, 1] = states[:, :width]
            send[0, part, 0, u] = transit.astype(B16)
            send[0, part, 1, u] = states[:, :width].astype(B16)
        copy(0, part).start()

    for r in range(rounds):
        part = step - 1 - r

        @pl.when((part >= 0) & (part < groups))
        def _():
            copy(r, part).wait_recv()
            upper = partner(r)[1] == 1
            for u in range(group):
                head = part * group + u
                got_e = recv[r, part, 1, u]
                if r == rounds - 1:
                    kept = carry[head] if r > 0 else None
                    far_state = mm(kept.astype(B16), got_e) if r > 0 else got_e.astype(F32)
                    cross[head, :, r * width : (r + 1) * width] = jnp.where(
                        upper, far_state, 0.0
                    ).astype(B16)
                    continue
                got_t = recv[r, part, 0, u]
                if r == 0:
                    a, b = places(width, width)
                    far_state = got_e.astype(F32)
                    moved = got_t.astype(F32)
                    kept = jnp.where(a == b, 1.0, 0.0)
                else:
                    kept = carry[head]
                    both = mm(kept.astype(B16), jnp.concatenate([got_t, got_e], -1))
                    moved, far_state = both[:, :width], both[:, width:]
                cross[head, :, r * width : (r + 1) * width] = jnp.where(
                    upper, far_state, 0.0
                ).astype(B16)
                carry[head] = jnp.where(upper, moved, kept)
                mine_t, mine_e = own[head, 0], own[head, 1]
                left = jnp.where(upper, mine_t, got_t.astype(F32)).astype(B16)
                right_t = jnp.where(upper, got_t.astype(F32), mine_t).astype(B16)
                right_e = jnp.where(upper, got_e.astype(F32), mine_e).astype(B16)
                later = jnp.where(upper, mine_e, got_e.astype(F32))
                joined = mm(left, jnp.concatenate([right_t, right_e], -1))
                new_t = joined[:, :width]
                new_e = joined[:, width:] + later
                own[head, 0] = new_t
                own[head, 1] = new_e
                send[r + 1, part, 0, u] = new_t.astype(B16)
                send[r + 1, part, 1, u] = new_e.astype(B16)
            if r < rounds - 1:
                copy(r + 1, part).start()

    @pl.when(step >= rounds)
    def _():
        part = step - rounds
        for u in range(group):
            head = part * group + u
            lanes = slice(u * width, (u + 1) * width)
            for r in range(rounds):
                rows[u, 2 + r : 3 + r, :] = weight_ref[1 + depth + r, pl.ds(head, 1), :]
            cols = rows[u].T
            far = mm(seen[head], cross[head])
            total = local[head]
            for r in range(rounds):
                total = total + cols[:, 2 + r : 3 + r] * far[:, r * width : (r + 1) * width]
            scaled = total * lax.rsqrt(jnp.mean(total * total, -1, keepdims=True) + 1e-06)
            o_ref[:, lanes] = (scaled * gain_ref[:, lanes]).astype(B16)

        for r in range(rounds):
            copy(r, part).wait_send()


def attention(query, keys, values, log_decay, beta, level_weights, norm_gain):
    tokens = query.shape[0]
    heads = log_decay.shape[0]
    width = query.shape[1] // heads
    levels = level_weights.shape[0]
    rounds = lax.axis_size("seq").bit_length() - 1
    depth = levels - 1 - rounds
    group = 2
    groups = heads // group

    def head_in(i):
        return (0, jnp.minimum(i, groups - 1))

    def head_out(i):
        return (0, jnp.maximum(i - rounds, 0))

    token_block = pl.BlockSpec((tokens, group * width), head_in)
    whole2 = pl.BlockSpec((heads, tokens), lambda i: (0, 0))
    return pl.pallas_call(
        functools.partial(attention_kernel, heads, group, rounds, depth),
        grid=(groups + rounds,),
        out_shape=jax.ShapeDtypeStruct((tokens, heads * width), B16),
        in_specs=[
            token_block, token_block, token_block, whole2, whole2,
            pl.BlockSpec((levels, heads, tokens), lambda i: (0, 0, 0)),
            pl.BlockSpec((1, group * width), head_out),
        ],
        out_specs=pl.BlockSpec((tokens, group * width), head_out),
        scratch_shapes=[
            pltpu.VMEM((heads, tokens), F32),
            pltpu.VMEM((group, 16, tokens), F32),
            pltpu.VMEM((heads, tokens, width), F32),
            pltpu.VMEM((heads, tokens, width), B16),
            pltpu.VMEM((heads, 2, width, width), F32),
            pltpu.VMEM((heads, width, width), F32),
            pltpu.VMEM((heads, width, rounds * width), B16),
            pltpu.VMEM((rounds, groups, 2, group, width, width), B16),
            pltpu.VMEM((rounds, groups, 2, group, width, width), B16),
            pltpu.SemaphoreType.DMA((rounds, groups)),
            pltpu.SemaphoreType.DMA((rounds, groups)),
        ],
        compiler_params=pltpu.CompilerParams(
            collective_id=0, has_side_effects=True, vmem_limit_bytes=60 << 20
        ),
    )(query, keys, values, log_decay, beta, level_weights, norm_gain.reshape(1, -1))


def project_kernel(
    span, chunks, n_ref, w_ref, o_ref, parts, send, recv, send_sem, recv_sem
):
    step = pl.program_id(0)
    me = lax.axis_index("head")
    rows = o_ref.shape[0]
    has_left, has_right = me > 0, me < span - 1

    def rightward(dest, chunk):
        return pltpu.make_async_remote_copy(
            src_ref=send.at[dest, chunk],
            dst_ref=recv.at[dest, chunk],
            send_sem=send_sem.at[dest, chunk],
            recv_sem=recv_sem.at[dest, chunk],
            device_id={"head": me + 1},
            device_id_type=MESH,
        )

    def leftward(dest, chunk, slot):
        return pltpu.make_async_remote_copy(
            src_ref=send.at[dest, chunk],
            dst_ref=recv.at[slot, chunk],
            send_sem=send_sem.at[dest, chunk],
            recv_sem=recv_sem.at[slot, chunk],
            device_id={"head": me - 1},
            device_id_type=MESH,
        )

    def leftward_slot(dest):
        return jnp.where(dest == me - 1, span, dest)

    @pl.when(step == 0)
    def _():
        barrier = pltpu.get_barrier_semaphore()

        @pl.when(has_left)
        def _():
            pl.semaphore_signal(barrier, inc=1, device_id={"head": me - 1}, device_id_type=MESH)

        @pl.when(has_right)
        def _():
            pl.semaphore_signal(barrier, inc=1, device_id={"head": me + 1}, device_id_type=MESH)

        neighbours = jnp.where(has_left, 1, 0) + jnp.where(has_right, 1, 0)
        pl.semaphore_wait(barrier, neighbours)

    @pl.when(step < chunks)
    def _():
        chunk = step
        parts[chunk] = mm(n_ref[...], w_ref[...])

        for dest in range(span - 1, 0, -1):
            @pl.when(me == 0)
            def _():
                send[dest, chunk] = parts[chunk, dest * rows : (dest + 1) * rows, :].astype(B16)

                @pl.when(chunk > 0)
                def _():
                    rightward(dest, chunk - 1).wait_send()

                rightward(dest, chunk).start()

        for dest in range(span - 1):
            @pl.when(me == span - 1)
            def _():
                send[dest, chunk] = parts[chunk, dest * rows : (dest + 1) * rows, :].astype(B16)

                @pl.when(chunk > 0)
                def _():
                    leftward(dest, chunk - 1, leftward_slot(dest)).wait_send()

                leftward(dest, chunk, leftward_slot(dest)).start()

    @pl.when(step >= chunks)
    def _():
        chunk = step - chunks

        for far in range(span - 1):
            right_dest, left_dest = span - 1 - far, far

            @pl.when(has_left & (right_dest > me))
            def _():
                rightward(right_dest, chunk).wait_recv()
                send[right_dest, chunk] = (
                    parts[chunk, right_dest * rows : (right_dest + 1) * rows, :]
                    + recv[right_dest, chunk].astype(F32)
                ).astype(B16)
                rightward(right_dest, chunk).start()

            @pl.when(has_right & (left_dest < me))
            def _():
                leftward(left_dest, chunk, left_dest).wait_recv()
                send[left_dest, chunk] = (
                    parts[chunk, left_dest * rows : (left_dest + 1) * rows, :]
                    + recv[left_dest, chunk].astype(F32)
                ).astype(B16)
                leftward(left_dest, chunk, leftward_slot(left_dest)).start()

        for dest in range(span):
            @pl.when(dest == me)
            def _():
                mine = parts[chunk, dest * rows : (dest + 1) * rows, :]
                if dest > 0:
                    rightward(dest, chunk).wait_recv()
                    mine = mine + recv[dest, chunk].astype(F32)
                if dest < span - 1:
                    leftward(dest, chunk, span).wait_recv()
                    mine = mine + recv[span, chunk].astype(F32)
                o_ref[...] = mine.astype(B16)

    @pl.when(step == 2 * chunks - 1)
    def _():
        @pl.loop(0, chunks)
        def _(chunk):
            for dest in range(span):
                left_over = (chunk == chunks - 1) | (has_left & has_right)

                @pl.when((dest > me) & left_over)
                def _():
                    rightward(dest, chunk).wait_send()

                @pl.when((dest < me) & left_over)
                def _():
                    leftward(dest, chunk, leftward_slot(dest)).wait_send()


def project(normed, out_weight):
    tokens, inner = normed.shape
    columns = out_weight.shape[1]
    span = lax.axis_size("head")
    rows = tokens // span
    piece = 512
    chunks = columns // piece
    return pl.pallas_call(
        functools.partial(project_kernel, span, chunks),
        grid=(2 * chunks,),
        out_shape=jax.ShapeDtypeStruct((rows, columns), B16),
        in_specs=[
            pl.BlockSpec((tokens, inner), lambda i: (0, 0)),
            pl.BlockSpec((inner, piece), lambda i: (0, jnp.minimum(i, chunks - 1))),
        ],
        out_specs=pl.BlockSpec((rows, piece), lambda i: (0, jnp.maximum(i - chunks, 0))),
        scratch_shapes=[
            pltpu.VMEM((chunks, tokens, piece), F32),
            pltpu.VMEM((span, chunks, rows, piece), B16),
            pltpu.VMEM((span + 1, chunks, rows, piece), B16),
            pltpu.SemaphoreType.DMA((span, chunks)),
            pltpu.SemaphoreType.DMA((span + 1, chunks)),
        ],
        compiler_params=pltpu.CompilerParams(
            collective_id=1, has_side_effects=True, vmem_limit_bytes=60 << 20
        ),
    )(normed, out_weight)


def per_device(query, keys, values, log_decay, beta, level_weights, norm_gain, out_weight):
    normed = attention(query, keys, values, log_decay, beta, level_weights, norm_gain)
    return project(normed, out_weight)


def solution(mesh):
    placed = (
        P("seq", "head"),
        P("seq", "head"),
        P("seq", "head"),
        P("head", "seq"),
        P("head", "seq"),
        P(None, "head", "seq"),
        P("head"),
        P("head", None),
    )
    return jax.shard_map(
        per_device, mesh=mesh, in_specs=placed, out_specs=P(("seq", "head"), None), check_vma=False
    )
```

```python
import functools

import jax
import jax.numpy as jnp
from jax import lax
from jax.experimental import pallas as pl
from jax.experimental.pallas import tpu as pltpu
from jax.sharding import PartitionSpec as P

BLK = 64
HALF = 256
MESH = pl.DeviceIdType.MESH
F32 = jnp.float32
B16 = jnp.bfloat16


def mm(left, right):
    return jnp.dot(left, right, preferred_element_type=F32)


def mm_t(left, right):
    return lax.dot_general(left, right, (((1,), (1,)), ((), ())), preferred_element_type=F32)


def mm_tl(left, right):
    return lax.dot_general(left, right, (((0,), (0,)), ((), ())), preferred_element_type=F32)


def unit_rows(matrix):
    return matrix * lax.rsqrt(jnp.sum(matrix * matrix, -1, keepdims=True) + 1e-06)


def places(rows, cols):
    return (
        lax.broadcasted_iota(jnp.int32, (rows, cols), 0),
        lax.broadcasted_iota(jnp.int32, (rows, cols), 1),
    )


def unit_lower_inverses(lowers):
    row, col = places(HALF, HALF)
    apart = row ^ col
    eye = jnp.where(row == col, 1.0, 0.0)
    ys = [jnp.where(apart < 16, -low, 0.0) for low in lowers]
    yb = [y.astype(B16) for y in ys]
    y2 = [mm(y, y) for y in yb]
    y2b = [y.astype(B16) for y in y2]
    y3 = [mm(y, z) for y, z in zip(yb, y2b)]
    y4b = [mm(y, y).astype(B16) for y in y2b]
    first = [eye + a + b + c for a, b, c in zip(ys, y2, y3)]
    y8b = [mm(y, y).astype(B16) for y in y4b]
    second = [a + mm(a.astype(B16), y) for a, y in zip(first, y4b)]
    xs = [a + mm(a.astype(B16), y) for a, y in zip(second, y8b)]
    size = 16
    while size < HALF:
        ring = (apart >= size) & (apart < 2 * size)
        xb = [x.astype(B16) for x in xs]
        inner = [
            mm(jnp.where(ring, low, 0.0).astype(B16), x).astype(B16) for low, x in zip(lowers, xb)
        ]
        xs = [x - mm(b, t) for x, b, t in zip(xs, xb, inner)]
        size *= 2
    return [x.astype(B16) for x in xs]


def attention_kernel(
    heads, group, rounds, depth,
    q_ref, k_ref, v_ref, decay_ref, beta_ref, weight_ref, gain_ref,
    o_ref,
    running, rows, local, seen, own, carry, cross, send, recv, send_sem, recv_sem,
):
    step = pl.program_id(0)
    me = lax.axis_index("seq")
    tokens = q_ref.shape[0]
    width = q_ref.shape[1] // group
    groups = heads // group

    def partner(r):
        bit = (me // (1 << r)) % 2
        return me + (1 - 2 * bit) * (1 << r), bit

    def copy(r, part):
        first = 1 if r == rounds - 1 else 0
        return pltpu.make_async_remote_copy(
            src_ref=send.at[r, part, pl.ds(first, 2 - first)],
            dst_ref=recv.at[r, part, pl.ds(first, 2 - first)],
            send_sem=send_sem.at[r, part],
            recv_sem=recv_sem.at[r, part],
            device_id={"seq": partner(r)[0]},
            device_id_type=MESH,
        )

    @pl.when(step == 0)
    def _():
        barrier = pltpu.get_barrier_semaphore()
        for r in range(rounds):
            pl.semaphore_signal(
                barrier, inc=1, device_id={"seq": partner(r)[0]}, device_id_type=MESH
            )
        pl.semaphore_wait(barrier, rounds)
        total = decay_ref[...]
        lane = lax.broadcasted_iota(jnp.int32, total.shape, 1)
        shift = 1
        while shift < tokens:
            total = total + jnp.where(lane >= shift, pltpu.roll(total, shift, 1), 0.0)
            shift *= 2
        running[...] = total
        rows[...] = jnp.zeros_like(rows)

    @pl.when(step < groups)
    def _():
        part = step
        row, col = places(HALF, HALF)
        apart = row ^ col
        on_below = row >= col
        below = row > col
        lo, hi = slice(0, HALF), slice(HALF, 2 * HALF)
        work = []
        for u in range(group):
            head = part * group + u
            rows[u, 0:1, :] = running[pl.ds(head, 1), :]
            rows[u, 1:2, :] = beta_ref[pl.ds(head, 1), :]
            for level in range(1 + depth):
                rows[u, 2 + level : 3 + level, :] = weight_ref[level, pl.ds(head, 1), :]
            run_row = rows[u, 0:1, :]
            cols = rows[u].T
            run = cols[:, 0:1]
            beta = cols[:, 1:2]
            gamma = jnp.exp(run)
            end = run[tokens - 1 : tokens, :]
            lanes = slice(u * width, (u + 1) * width)
            qn = unit_rows(q_ref[:, lanes].astype(F32))
            kn = unit_rows(k_ref[:, lanes].astype(F32))
            qb = qn.astype(B16)
            kb = kn.astype(B16)
            fresh = (beta * v_ref[:, lanes].astype(F32)).astype(B16)
            faded = (beta * gamma * kn).astype(B16)
            pair = jnp.concatenate([fresh, faded], -1)
            tail = (jnp.exp(end - run) * kn).astype(B16)

            def decay(i, j):
                gap = jnp.exp(jnp.minimum(run[i] - run_row[:, j], 0.0))
                return jnp.where(on_below, gap, 0.0) if i == j else gap

            d00, d10, d11 = decay(lo, lo), decay(hi, lo), decay(hi, hi)
            l00 = jnp.where(below, beta[lo] * d00 * mm_t(kb[lo], kb[lo]), 0.0)
            l11 = jnp.where(below, beta[hi] * d11 * mm_t(kb[hi], kb[hi]), 0.0)
            l10 = (beta[hi] * d10 * mm_t(kb[hi], kb[lo])).astype(B16)
            m00 = (d00 * mm_t(qb[lo], kb[lo])).astype(B16)
            m11 = (d11 * mm_t(qb[hi], kb[hi])).astype(B16)
            m10 = (d10 * mm_t(qb[hi], kb[lo])).astype(B16)
            work.append((cols, gamma, end, qn, fresh, faded, pair, tail, l00, l11, l10, m00, m11, m10))
        inverses = unit_lower_inverses([low for item in work for low in item[8:10]])
        x10s = [
            mm(item[10], inverses[2 * u]).astype(B16) for u, item in enumerate(work)
        ]
        x10s = [(-mm(inverses[2 * u + 1], x)).astype(B16) for u, x in enumerate(x10s)]
        for u, item in enumerate(work):
            head = part * group + u
            cols, gamma, end, qn, fresh, faded, pair, tail, _, _, _, m00, m11, m10 = item
            x00, x11, x10 = inverses[2 * u], inverses[2 * u + 1], x10s[u]
            p00 = mm(m00, x00)
            p11 = mm(m11, x11)
            p10 = (mm(m10, x00) + mm(m11, x10)).astype(B16)

            def level_weight(i):
                chosen = cols[i, 1 + depth : 2 + depth]
                for level in range(depth - 2, -1, -1):
                    chosen = jnp.where(apart < (BLK << level), cols[i, 2 + level : 3 + level], chosen)
                return chosen

            both = mm(p10, pair[lo])
            local[head, lo, :] = mm((level_weight(lo) * p00).astype(B16), fresh[lo])
            local[head, hi, :] = (
                mm((level_weight(hi) * p11).astype(B16), fresh[hi])
                + cols[hi, 2 + depth : 3 + depth] * both[:, :width]
            )
            seen[head, lo, :] = (gamma[lo] * qn[lo] - mm(p00.astype(B16), faded[lo])).astype(B16)
            seen[head, hi, :] = (
                gamma[hi] * qn[hi] - both[:, width:] - mm(p11.astype(B16), faded[hi])
            ).astype(B16)
            r0 = (mm_tl(tail[lo], x00) + mm_tl(tail[hi], x10)).astype(B16)
            r1 = mm_tl(tail[hi], x11).astype(B16)
            states = mm(r0, pair[lo]) + mm(r1, pair[hi])
            a, b = places(width, width)
            transit = jnp.where(a == b, jnp.exp(end), 0.0) - states[:, width:]
            own[head, 0] = transit
            own[head, 1] = states[:, :width]
            send[0, part, 0, u] = transit.astype(B16)
            send[0, part, 1, u] = states[:, :width].astype(B16)
        copy(0, part).start()

    for r in range(rounds):
        part = step - 1 - r

        @pl.when((part >= 0) & (part < groups))
        def _():
            copy(r, part).wait_recv()
            upper = partner(r)[1] == 1
            for u in range(group):
                head = part * group + u
                got_e = recv[r, part, 1, u]
                if r == rounds - 1:
                    kept = carry[head] if r > 0 else None
                    far_state = mm(kept.astype(B16), got_e) if r > 0 else got_e.astype(F32)
                    cross[head, :, r * width : (r + 1) * width] = jnp.where(
                        upper, far_state, 0.0
                    ).astype(B16)
                    continue
                got_t = recv[r, part, 0, u]
                if r == 0:
                    a, b = places(width, width)
                    far_state = got_e.astype(F32)
                    moved = got_t.astype(F32)
                    kept = jnp.where(a == b, 1.0, 0.0)
                else:
                    kept = carry[head]
                    both = mm(kept.astype(B16), jnp.concatenate([got_t, got_e], -1))
                    moved, far_state = both[:, :width], both[:, width:]
                cross[head, :, r * width : (r + 1) * width] = jnp.where(
                    upper, far_state, 0.0
                ).astype(B16)
                carry[head] = jnp.where(upper, moved, kept)
                mine_t, mine_e = own[head, 0], own[head, 1]
                left = jnp.where(upper, mine_t, got_t.astype(F32)).astype(B16)
                right_t = jnp.where(upper, got_t.astype(F32), mine_t).astype(B16)
                right_e = jnp.where(upper, got_e.astype(F32), mine_e).astype(B16)
                later = jnp.where(upper, mine_e, got_e.astype(F32))
                joined = mm(left, jnp.concatenate([right_t, right_e], -1))
                new_t = joined[:, :width]
                new_e = joined[:, width:] + later
                own[head, 0] = new_t
                own[head, 1] = new_e
                send[r + 1, part, 0, u] = new_t.astype(B16)
                send[r + 1, part, 1, u] = new_e.astype(B16)
            if r < rounds - 1:
                copy(r + 1, part).start()

    @pl.when(step >= rounds)
    def _():
        part = step - rounds
        for u in range(group):
            head = part * group + u
            lanes = slice(u * width, (u + 1) * width)
            for r in range(rounds):
                rows[u, 2 + r : 3 + r, :] = weight_ref[1 + depth + r, pl.ds(head, 1), :]
            cols = rows[u].T
            far = mm(seen[head], cross[head])
            total = local[head]
            for r in range(rounds):
                total = total + cols[:, 2 + r : 3 + r] * far[:, r * width : (r + 1) * width]
            scaled = total * lax.rsqrt(jnp.mean(total * total, -1, keepdims=True) + 1e-06)
            o_ref[:, lanes] = (scaled * gain_ref[:, lanes]).astype(B16)

        for r in range(rounds):
            copy(r, part).wait_send()


def attention(query, keys, values, log_decay, beta, level_weights, norm_gain):
    tokens = query.shape[0]
    heads = log_decay.shape[0]
    width = query.shape[1] // heads
    levels = level_weights.shape[0]
    rounds = lax.axis_size("seq").bit_length() - 1
    depth = levels - 1 - rounds
    group = 4 if heads % 4 == 0 else 1
    groups = heads // group

    def head_in(i):
        return (0, jnp.minimum(i, groups - 1))

    def head_out(i):
        return (0, jnp.maximum(i - rounds, 0))

    token_block = pl.BlockSpec((tokens, group * width), head_in)
    whole2 = pl.BlockSpec((heads, tokens), lambda i: (0, 0))
    return pl.pallas_call(
        functools.partial(attention_kernel, heads, group, rounds, depth),
        grid=(groups + rounds,),
        out_shape=jax.ShapeDtypeStruct((tokens, heads * width), B16),
        in_specs=[
            token_block, token_block, token_block, whole2, whole2,
            pl.BlockSpec((levels, heads, tokens), lambda i: (0, 0, 0)),
            pl.BlockSpec((1, group * width), head_out),
        ],
        out_specs=pl.BlockSpec((tokens, group * width), head_out),
        scratch_shapes=[
            pltpu.VMEM((heads, tokens), F32),
            pltpu.VMEM((group, 16, tokens), F32),
            pltpu.VMEM((heads, tokens, width), F32),
            pltpu.VMEM((heads, tokens, width), B16),
            pltpu.VMEM((heads, 2, width, width), F32),
            pltpu.VMEM((heads, width, width), F32),
            pltpu.VMEM((heads, width, rounds * width), B16),
            pltpu.VMEM((rounds, groups, 2, group, width, width), B16),
            pltpu.VMEM((rounds, groups, 2, group, width, width), B16),
            pltpu.SemaphoreType.DMA((rounds, groups)),
            pltpu.SemaphoreType.DMA((rounds, groups)),
        ],
        compiler_params=pltpu.CompilerParams(
            collective_id=0, has_side_effects=True, vmem_limit_bytes=60 << 20
        ),
    )(query, keys, values, log_decay, beta, level_weights, norm_gain.reshape(1, -1))


def project_kernel(
    span, chunks, n_ref, w_ref, o_ref, parts, send, recv, send_sem, recv_sem
):
    step = pl.program_id(0)
    me = lax.axis_index("head")
    rows = o_ref.shape[0]
    has_left, has_right = me > 0, me < span - 1

    def rightward(dest, chunk):
        return pltpu.make_async_remote_copy(
            src_ref=send.at[dest, chunk],
            dst_ref=recv.at[dest, chunk],
            send_sem=send_sem.at[dest, chunk],
            recv_sem=recv_sem.at[dest, chunk],
            device_id={"head": me + 1},
            device_id_type=MESH,
        )

    def leftward(dest, chunk, slot):
        return pltpu.make_async_remote_copy(
            src_ref=send.at[dest, chunk],
            dst_ref=recv.at[slot, chunk],
            send_sem=send_sem.at[dest, chunk],
            recv_sem=recv_sem.at[slot, chunk],
            device_id={"head": me - 1},
            device_id_type=MESH,
        )

    def leftward_slot(dest):
        return jnp.where(dest == me - 1, span, dest)

    @pl.when(step == 0)
    def _():
        barrier = pltpu.get_barrier_semaphore()

        @pl.when(has_left)
        def _():
            pl.semaphore_signal(barrier, inc=1, device_id={"head": me - 1}, device_id_type=MESH)

        @pl.when(has_right)
        def _():
            pl.semaphore_signal(barrier, inc=1, device_id={"head": me + 1}, device_id_type=MESH)

        neighbours = jnp.where(has_left, 1, 0) + jnp.where(has_right, 1, 0)
        pl.semaphore_wait(barrier, neighbours)

    @pl.when(step < chunks)
    def _():
        chunk = step
        parts[chunk] = mm(n_ref[...], w_ref[...])

        for dest in range(span - 1, 0, -1):
            @pl.when(me == 0)
            def _():
                send[dest, chunk] = parts[chunk, dest * rows : (dest + 1) * rows, :].astype(B16)

                @pl.when(chunk > 0)
                def _():
                    rightward(dest, chunk - 1).wait_send()

                rightward(dest, chunk).start()

        for dest in range(span - 1):
            @pl.when(me == span - 1)
            def _():
                send[dest, chunk] = parts[chunk, dest * rows : (dest + 1) * rows, :].astype(B16)

                @pl.when(chunk > 0)
                def _():
                    leftward(dest, chunk - 1, leftward_slot(dest)).wait_send()

                leftward(dest, chunk, leftward_slot(dest)).start()

    @pl.when(step >= chunks)
    def _():
        chunk = step - chunks

        for far in range(span - 1):
            right_dest, left_dest = span - 1 - far, far

            @pl.when(has_left & (right_dest > me))
            def _():
                rightward(right_dest, chunk).wait_recv()
                send[right_dest, chunk] = (
                    parts[chunk, right_dest * rows : (right_dest + 1) * rows, :]
                    + recv[right_dest, chunk].astype(F32)
                ).astype(B16)
                rightward(right_dest, chunk).start()

            @pl.when(has_right & (left_dest < me))
            def _():
                leftward(left_dest, chunk, left_dest).wait_recv()
                send[left_dest, chunk] = (
                    parts[chunk, left_dest * rows : (left_dest + 1) * rows, :]
                    + recv[left_dest, chunk].astype(F32)
                ).astype(B16)
                leftward(left_dest, chunk, leftward_slot(left_dest)).start()

        for dest in range(span):
            @pl.when(dest == me)
            def _():
                mine = parts[chunk, dest * rows : (dest + 1) * rows, :]
                if dest > 0:
                    rightward(dest, chunk).wait_recv()
                    mine = mine + recv[dest, chunk].astype(F32)
                if dest < span - 1:
                    leftward(dest, chunk, span).wait_recv()
                    mine = mine + recv[span, chunk].astype(F32)
                o_ref[...] = mine.astype(B16)

    @pl.when(step == 2 * chunks - 1)
    def _():
        @pl.loop(0, chunks)
        def _(chunk):
            for dest in range(span):
                left_over = (chunk == chunks - 1) | (has_left & has_right)

                @pl.when((dest > me) & left_over)
                def _():
                    rightward(dest, chunk).wait_send()

                @pl.when((dest < me) & left_over)
                def _():
                    leftward(dest, chunk, leftward_slot(dest)).wait_send()


def project(normed, out_weight):
    tokens, inner = normed.shape
    columns = out_weight.shape[1]
    span = lax.axis_size("head")
    rows = tokens // span
    piece = 512
    chunks = columns // piece
    return pl.pallas_call(
        functools.partial(project_kernel, span, chunks),
        grid=(2 * chunks,),
        out_shape=jax.ShapeDtypeStruct((rows, columns), B16),
        in_specs=[
            pl.BlockSpec((tokens, inner), lambda i: (0, 0)),
            pl.BlockSpec((inner, piece), lambda i: (0, jnp.minimum(i, chunks - 1))),
        ],
        out_specs=pl.BlockSpec((rows, piece), lambda i: (0, jnp.maximum(i - chunks, 0))),
        scratch_shapes=[
            pltpu.VMEM((chunks, tokens, piece), F32),
            pltpu.VMEM((span, chunks, rows, piece), B16),
            pltpu.VMEM((span + 1, chunks, rows, piece), B16),
            pltpu.SemaphoreType.DMA((span, chunks)),
            pltpu.SemaphoreType.DMA((span + 1, chunks)),
        ],
        compiler_params=pltpu.CompilerParams(
            collective_id=1, has_side_effects=True, vmem_limit_bytes=60 << 20
        ),
    )(normed, out_weight)


def per_device(query, keys, values, log_decay, beta, level_weights, norm_gain, out_weight):
    normed = attention(query, keys, values, log_decay, beta, level_weights, norm_gain)
    return project(normed, out_weight)


def solution(mesh):
    placed = (
        P("seq", "head"),
        P("seq", "head"),
        P("seq", "head"),
        P("head", "seq"),
        P("head", "seq"),
        P(None, "head", "seq"),
        P("head"),
        P("head", None),
    )
    return jax.shard_map(
        per_device, mesh=mesh, in_specs=placed, out_specs=P(("seq", "head"), None), check_vma=False
    )
```

```python
import functools

import jax
import jax.numpy as jnp
from jax import lax
from jax.experimental import pallas as pl
from jax.experimental.pallas import tpu as pltpu
from jax.sharding import PartitionSpec as P

BLK = 64
HALF = 256
MESH = pl.DeviceIdType.MESH
F32 = jnp.float32
B16 = jnp.bfloat16


def mm(left, right):
    return jnp.dot(left, right, preferred_element_type=F32)


def mm_t(left, right):
    return lax.dot_general(left, right, (((1,), (1,)), ((), ())), preferred_element_type=F32)


def mm_tl(left, right):
    return lax.dot_general(left, right, (((0,), (0,)), ((), ())), preferred_element_type=F32)


def unit_rows(matrix):
    return matrix * lax.rsqrt(jnp.sum(matrix * matrix, -1, keepdims=True) + 1e-06)


def places(rows, cols):
    return (
        lax.broadcasted_iota(jnp.int32, (rows, cols), 0),
        lax.broadcasted_iota(jnp.int32, (rows, cols), 1),
    )


def unit_lower_inverses(lowers):
    row, col = places(HALF, HALF)
    apart = row ^ col
    eye = jnp.where(row == col, 1.0, 0.0)
    ys = [jnp.where(apart < 16, -low, 0.0) for low in lowers]
    yb = [y.astype(B16) for y in ys]
    y2 = [mm(y, y) for y in yb]
    y2b = [y.astype(B16) for y in y2]
    y3 = [mm(y, z) for y, z in zip(yb, y2b)]
    y4b = [mm(y, y).astype(B16) for y in y2b]
    first = [eye + a + b + c for a, b, c in zip(ys, y2, y3)]
    y8b = [mm(y, y).astype(B16) for y in y4b]
    second = [a + mm(a.astype(B16), y) for a, y in zip(first, y4b)]
    xs = [a + mm(a.astype(B16), y) for a, y in zip(second, y8b)]
    size = 16
    while size < HALF:
        ring = (apart >= size) & (apart < 2 * size)
        xb = [x.astype(B16) for x in xs]
        inner = [
            mm(jnp.where(ring, low, 0.0).astype(B16), x).astype(B16) for low, x in zip(lowers, xb)
        ]
        xs = [x - mm(b, t) for x, b, t in zip(xs, xb, inner)]
        size *= 2
    return [x.astype(B16) for x in xs]


def attention_kernel(
    heads, group, rounds, depth,
    q_ref, k_ref, v_ref, decay_ref, beta_ref, weight_ref, gain_ref,
    o_ref,
    running, rows, local, seen, own, carry, cross, send, recv, send_sem, recv_sem,
):
    step = pl.program_id(0)
    me = lax.axis_index("seq")
    tokens = q_ref.shape[0]
    width = q_ref.shape[1] // group
    groups = heads // group

    def partner(r):
        bit = (me // (1 << r)) % 2
        return me + (1 - 2 * bit) * (1 << r), bit

    def copy(r, part):
        first = 1 if r == rounds - 1 else 0
        return pltpu.make_async_remote_copy(
            src_ref=send.at[r, part, pl.ds(first, 2 - first)],
            dst_ref=recv.at[r, part, pl.ds(first, 2 - first)],
            send_sem=send_sem.at[r, part],
            recv_sem=recv_sem.at[r, part],
            device_id={"seq": partner(r)[0]},
            device_id_type=MESH,
        )

    @pl.when(step == 0)
    def _():
        barrier = pltpu.get_barrier_semaphore()
        for r in range(rounds):
            pl.semaphore_signal(
                barrier, inc=1, device_id={"seq": partner(r)[0]}, device_id_type=MESH
            )
        pl.semaphore_wait(barrier, rounds)
        total = decay_ref[...]
        lane = lax.broadcasted_iota(jnp.int32, total.shape, 1)
        shift = 1
        while shift < tokens:
            total = total + jnp.where(lane >= shift, pltpu.roll(total, shift, 1), 0.0)
            shift *= 2
        running[...] = total
        rows[...] = jnp.zeros_like(rows)

    @pl.when(step < groups)
    def _():
        part = step
        row, col = places(HALF, HALF)
        apart = row ^ col
        on_below = row >= col
        below = row > col
        lo, hi = slice(0, HALF), slice(HALF, 2 * HALF)
        work = []
        for u in range(group):
            head = part * group + u
            rows[u, 0:1, :] = running[pl.ds(head, 1), :]
            rows[u, 1:2, :] = beta_ref[pl.ds(head, 1), :]
            for level in range(1 + depth):
                rows[u, 2 + level : 3 + level, :] = weight_ref[level, pl.ds(head, 1), :]
            run_row = rows[u, 0:1, :]
            cols = rows[u].T
            run = cols[:, 0:1]
            beta = cols[:, 1:2]
            gamma = jnp.exp(run)
            end = run[tokens - 1 : tokens, :]
            lanes = slice(u * width, (u + 1) * width)
            qn = unit_rows(q_ref[:, lanes].astype(F32))
            kn = unit_rows(k_ref[:, lanes].astype(F32))
            qb = qn.astype(B16)
            kb = kn.astype(B16)
            fresh = (beta * v_ref[:, lanes].astype(F32)).astype(B16)
            faded = (beta * gamma * kn).astype(B16)
            pair = jnp.concatenate([fresh, faded], -1)
            tail = (jnp.exp(end - run) * kn).astype(B16)

            def decay(i, j):
                gap = jnp.exp(jnp.minimum(run[i] - run_row[:, j], 0.0))
                return jnp.where(on_below, gap, 0.0) if i == j else gap

            d00, d10, d11 = decay(lo, lo), decay(hi, lo), decay(hi, hi)
            l00 = jnp.where(below, beta[lo] * d00 * mm_t(kb[lo], kb[lo]), 0.0)
            l11 = jnp.where(below, beta[hi] * d11 * mm_t(kb[hi], kb[hi]), 0.0)
            l10 = (beta[hi] * d10 * mm_t(kb[hi], kb[lo])).astype(B16)
            m00 = (d00 * mm_t(qb[lo], kb[lo])).astype(B16)
            m11 = (d11 * mm_t(qb[hi], kb[hi])).astype(B16)
            m10 = (d10 * mm_t(qb[hi], kb[lo])).astype(B16)
            work.append((cols, gamma, end, qn, fresh, faded, pair, tail, l00, l11, l10, m00, m11, m10))
        inverses = unit_lower_inverses([low for item in work for low in item[8:10]])
        x10s = [
            mm(item[10], inverses[2 * u]).astype(B16) for u, item in enumerate(work)
        ]
        x10s = [(-mm(inverses[2 * u + 1], x)).astype(B16) for u, x in enumerate(x10s)]
        for u, item in enumerate(work):
            head = part * group + u
            cols, gamma, end, qn, fresh, faded, pair, tail, _, _, _, m00, m11, m10 = item
            x00, x11, x10 = inverses[2 * u], inverses[2 * u + 1], x10s[u]
            p00 = mm(m00, x00)
            p11 = mm(m11, x11)
            p10 = (mm(m10, x00) + mm(m11, x10)).astype(B16)

            def level_weight(i):
                chosen = cols[i, 1 + depth : 2 + depth]
                for level in range(depth - 2, -1, -1):
                    chosen = jnp.where(apart < (BLK << level), cols[i, 2 + level : 3 + level], chosen)
                return chosen

            both = mm(p10, pair[lo])
            local[head, lo, :] = mm((level_weight(lo) * p00).astype(B16), fresh[lo])
            local[head, hi, :] = (
                mm((level_weight(hi) * p11).astype(B16), fresh[hi])
                + cols[hi, 2 + depth : 3 + depth] * both[:, :width]
            )
            seen[head, lo, :] = (gamma[lo] * qn[lo] - mm(p00.astype(B16), faded[lo])).astype(B16)
            seen[head, hi, :] = (
                gamma[hi] * qn[hi] - both[:, width:] - mm(p11.astype(B16), faded[hi])
            ).astype(B16)
            r0 = (mm_tl(tail[lo], x00) + mm_tl(tail[hi], x10)).astype(B16)
            r1 = mm_tl(tail[hi], x11).astype(B16)
            states = mm(r0, pair[lo]) + mm(r1, pair[hi])
            a, b = places(width, width)
            transit = jnp.where(a == b, jnp.exp(end), 0.0) - states[:, width:]
            own[head, 0] = transit
            own[head, 1] = states[:, :width]
            send[0, part, 0, u] = transit.astype(B16)
            send[0, part, 1, u] = states[:, :width].astype(B16)
        copy(0, part).start()

    for r in range(rounds):
        part = step - 1 - r

        @pl.when((part >= 0) & (part < groups))
        def _():
            copy(r, part).wait_recv()
            upper = partner(r)[1] == 1
            for u in range(group):
                head = part * group + u
                got_e = recv[r, part, 1, u]
                if r == rounds - 1:
                    kept = carry[head] if r > 0 else None
                    far_state = mm(kept.astype(B16), got_e) if r > 0 else got_e.astype(F32)
                    cross[head, :, r * width : (r + 1) * width] = jnp.where(
                        upper, far_state, 0.0
                    ).astype(B16)
                    continue
                got_t = recv[r, part, 0, u]
                if r == 0:
                    a, b = places(width, width)
                    far_state = got_e.astype(F32)
                    moved = got_t.astype(F32)
                    kept = jnp.where(a == b, 1.0, 0.0)
                else:
                    kept = carry[head]
                    both = mm(kept.astype(B16), jnp.concatenate([got_t, got_e], -1))
                    moved, far_state = both[:, :width], both[:, width:]
                cross[head, :, r * width : (r + 1) * width] = jnp.where(
                    upper, far_state, 0.0
                ).astype(B16)
                carry[head] = jnp.where(upper, moved, kept)
                mine_t, mine_e = own[head, 0], own[head, 1]
                left = jnp.where(upper, mine_t, got_t.astype(F32)).astype(B16)
                right_t = jnp.where(upper, got_t.astype(F32), mine_t).astype(B16)
                right_e = jnp.where(upper, got_e.astype(F32), mine_e).astype(B16)
                later = jnp.where(upper, mine_e, got_e.astype(F32))
                joined = mm(left, jnp.concatenate([right_t, right_e], -1))
                new_t = joined[:, :width]
                new_e = joined[:, width:] + later
                own[head, 0] = new_t
                own[head, 1] = new_e
                send[r + 1, part, 0, u] = new_t.astype(B16)
                send[r + 1, part, 1, u] = new_e.astype(B16)
            if r < rounds - 1:
                copy(r + 1, part).start()

    @pl.when(step >= rounds)
    def _():
        part = step - rounds
        for u in range(group):
            head = part * group + u
            lanes = slice(u * width, (u + 1) * width)
            for r in range(rounds):
                rows[u, 2 + r : 3 + r, :] = weight_ref[1 + depth + r, pl.ds(head, 1), :]
            cols = rows[u].T
            far = mm(seen[head], cross[head])
            total = local[head]
            for r in range(rounds):
                total = total + cols[:, 2 + r : 3 + r] * far[:, r * width : (r + 1) * width]
            scaled = total * lax.rsqrt(jnp.mean(total * total, -1, keepdims=True) + 1e-06)
            o_ref[:, lanes] = (scaled * gain_ref[:, lanes]).astype(B16)

        for r in range(rounds):
            copy(r, part).wait_send()


def attention(query, keys, values, log_decay, beta, level_weights, norm_gain):
    tokens = query.shape[0]
    heads = log_decay.shape[0]
    width = query.shape[1] // heads
    levels = level_weights.shape[0]
    rounds = lax.axis_size("seq").bit_length() - 1
    depth = levels - 1 - rounds
    group = 2
    groups = heads // group

    def head_in(i):
        return (0, jnp.minimum(i, groups - 1))

    def head_out(i):
        return (0, jnp.maximum(i - rounds, 0))

    token_block = pl.BlockSpec((tokens, group * width), head_in)
    whole2 = pl.BlockSpec((heads, tokens), lambda i: (0, 0))
    return pl.pallas_call(
        functools.partial(attention_kernel, heads, group, rounds, depth),
        grid=(groups + rounds,),
        out_shape=jax.ShapeDtypeStruct((tokens, heads * width), B16),
        in_specs=[
            token_block, token_block, token_block, whole2, whole2,
            pl.BlockSpec((levels, heads, tokens), lambda i: (0, 0, 0)),
            pl.BlockSpec((1, group * width), head_out),
        ],
        out_specs=pl.BlockSpec((tokens, group * width), head_out),
        scratch_shapes=[
            pltpu.VMEM((heads, tokens), F32),
            pltpu.VMEM((group, 16, tokens), F32),
            pltpu.VMEM((heads, tokens, width), F32),
            pltpu.VMEM((heads, tokens, width), B16),
            pltpu.VMEM((heads, 2, width, width), F32),
            pltpu.VMEM((heads, width, width), F32),
            pltpu.VMEM((heads, width, rounds * width), B16),
            pltpu.VMEM((rounds, groups, 2, group, width, width), B16),
            pltpu.VMEM((rounds, groups, 2, group, width, width), B16),
            pltpu.SemaphoreType.DMA((rounds, groups)),
            pltpu.SemaphoreType.DMA((rounds, groups)),
        ],
        compiler_params=pltpu.CompilerParams(
            collective_id=0, has_side_effects=True, vmem_limit_bytes=60 << 20
        ),
    )(query, keys, values, log_decay, beta, level_weights, norm_gain.reshape(1, -1))


def project_kernel(
    span, chunks, n_ref, w_ref, o_ref, parts, send, recv, send_sem, recv_sem
):
    step = pl.program_id(0)
    me = lax.axis_index("head")
    rows = o_ref.shape[0]
    has_left, has_right = me > 0, me < span - 1

    def rightward(dest, chunk):
        return pltpu.make_async_remote_copy(
            src_ref=send.at[dest, chunk],
            dst_ref=recv.at[dest, chunk],
            send_sem=send_sem.at[dest, chunk],
            recv_sem=recv_sem.at[dest, chunk],
            device_id={"head": me + 1},
            device_id_type=MESH,
        )

    def leftward(dest, chunk, slot):
        return pltpu.make_async_remote_copy(
            src_ref=send.at[dest, chunk],
            dst_ref=recv.at[slot, chunk],
            send_sem=send_sem.at[dest, chunk],
            recv_sem=recv_sem.at[slot, chunk],
            device_id={"head": me - 1},
            device_id_type=MESH,
        )

    def leftward_slot(dest):
        return jnp.where(dest == me - 1, span, dest)

    @pl.when(step == 0)
    def _():
        barrier = pltpu.get_barrier_semaphore()

        @pl.when(has_left)
        def _():
            pl.semaphore_signal(barrier, inc=1, device_id={"head": me - 1}, device_id_type=MESH)

        @pl.when(has_right)
        def _():
            pl.semaphore_signal(barrier, inc=1, device_id={"head": me + 1}, device_id_type=MESH)

        neighbours = jnp.where(has_left, 1, 0) + jnp.where(has_right, 1, 0)
        pl.semaphore_wait(barrier, neighbours)

    @pl.when(step < chunks)
    def _():
        chunk = step
        parts[chunk] = mm(n_ref[...], w_ref[...])

        for dest in range(span - 1, 0, -1):
            @pl.when(me == 0)
            def _():
                send[dest, chunk] = parts[chunk, dest * rows : (dest + 1) * rows, :].astype(B16)

                @pl.when(chunk > 0)
                def _():
                    rightward(dest, chunk - 1).wait_send()

                rightward(dest, chunk).start()

        for dest in range(span - 1):
            @pl.when(me == span - 1)
            def _():
                send[dest, chunk] = parts[chunk, dest * rows : (dest + 1) * rows, :].astype(B16)

                @pl.when(chunk > 0)
                def _():
                    leftward(dest, chunk - 1, leftward_slot(dest)).wait_send()

                leftward(dest, chunk, leftward_slot(dest)).start()

    @pl.when(step >= chunks)
    def _():
        chunk = step - chunks

        for far in range(span - 1):
            right_dest, left_dest = span - 1 - far, far

            @pl.when(has_left & (right_dest > me))
            def _():
                rightward(right_dest, chunk).wait_recv()
                send[right_dest, chunk] = (
                    parts[chunk, right_dest * rows : (right_dest + 1) * rows, :]
                    + recv[right_dest, chunk].astype(F32)
                ).astype(B16)
                rightward(right_dest, chunk).start()

            @pl.when(has_right & (left_dest < me))
            def _():
                leftward(left_dest, chunk, left_dest).wait_recv()
                send[left_dest, chunk] = (
                    parts[chunk, left_dest * rows : (left_dest + 1) * rows, :]
                    + recv[left_dest, chunk].astype(F32)
                ).astype(B16)
                leftward(left_dest, chunk, leftward_slot(left_dest)).start()

        for dest in range(span):
            @pl.when(dest == me)
            def _():
                mine = parts[chunk, dest * rows : (dest + 1) * rows, :]
                if dest > 0:
                    rightward(dest, chunk).wait_recv()
                    mine = mine + recv[dest, chunk].astype(F32)
                if dest < span - 1:
                    leftward(dest, chunk, span).wait_recv()
                    mine = mine + recv[span, chunk].astype(F32)
                o_ref[...] = mine.astype(B16)

    @pl.when(step == 2 * chunks - 1)
    def _():
        @pl.loop(0, chunks)
        def _(chunk):
            for dest in range(span):
                left_over = (chunk == chunks - 1) | (has_left & has_right)

                @pl.when((dest > me) & left_over)
                def _():
                    rightward(dest, chunk).wait_send()

                @pl.when((dest < me) & left_over)
                def _():
                    leftward(dest, chunk, leftward_slot(dest)).wait_send()


def project(normed, out_weight):
    tokens, inner = normed.shape
    columns = out_weight.shape[1]
    span = lax.axis_size("head")
    rows = tokens // span
    piece = 256
    chunks = columns // piece
    return pl.pallas_call(
        functools.partial(project_kernel, span, chunks),
        grid=(2 * chunks,),
        out_shape=jax.ShapeDtypeStruct((rows, columns), B16),
        in_specs=[
            pl.BlockSpec((tokens, inner), lambda i: (0, 0)),
            pl.BlockSpec((inner, piece), lambda i: (0, jnp.minimum(i, chunks - 1))),
        ],
        out_specs=pl.BlockSpec((rows, piece), lambda i: (0, jnp.maximum(i - chunks, 0))),
        scratch_shapes=[
            pltpu.VMEM((chunks, tokens, piece), F32),
            pltpu.VMEM((span, chunks, rows, piece), B16),
            pltpu.VMEM((span + 1, chunks, rows, piece), B16),
            pltpu.SemaphoreType.DMA((span, chunks)),
            pltpu.SemaphoreType.DMA((span + 1, chunks)),
        ],
        compiler_params=pltpu.CompilerParams(
            collective_id=1, has_side_effects=True, vmem_limit_bytes=60 << 20
        ),
    )(normed, out_weight)


def per_device(query, keys, values, log_decay, beta, level_weights, norm_gain, out_weight):
    normed = attention(query, keys, values, log_decay, beta, level_weights, norm_gain)
    return project(normed, out_weight)


def solution(mesh):
    placed = (
        P("seq", "head"),
        P("seq", "head"),
        P("seq", "head"),
        P("head", "seq"),
        P("head", "seq"),
        P(None, "head", "seq"),
        P("head"),
        P("head", None),
    )
    return jax.shard_map(
        per_device, mesh=mesh, in_specs=placed, out_specs=P(("seq", "head"), None), check_vma=False
    )
```
